256 devices in a mesh: span: 64 (over x, z, core), row: 4 (over y).
Axes of the slice: x: 4, y: 4, z: 8, core: 2. Of those that a mesh axis runs over, the one named last changes fastest.
Arguments:
- features: bfloat16 [64, 4, 32, 32, 128], P('span', None, 'row'), may hold values from -6 to 6
- clip_lengths: int32 [16], replicated, may hold values from 1 to 32, 64 in all
- clip_order: int32 [16], replicated, may hold values from 0 to 15, each once
- weight_a: bfloat16 [3, 3, 3, 128, 128], replicated, may hold values from -0.109375 to 0.109375
- bias_a: float32 [128], replicated, may hold values from -3 to 3
- weight_b: bfloat16 [3, 3, 3, 128, 128], replicated, may hold values from -0.109375 to 0.109375
- bias_b: float32 [128], replicated, may hold values from -3 to 3
- weight_down: bfloat16 [3, 3, 3, 128, 128], replicated, may hold values from -0.109375 to 0.109375
- bias_down: float32 [128], replicated, may hold values from -3 to 3
Outputs:
- patch_tokens: bfloat16 [64, 2, 8, 8, 512], P('span', None, 'row')
The draws below stay inside these ranges and needn't reach their ends.
Inputs may be any that keep to these rules, and one draw needn't show every extreme that they name: `clip_lengths`: the lengths sum to 64. `clip_order`: each clip appears once.
All inputs are finite; a program needn't handle non-finite values.
Results may differ from the reference program's by a relative error of at most 0.0051.
Values may be sent and summed in bfloat16 or wider, within the bound.
No kernel may reach another device: no remote copies, remote signals or barrier semaphores. Data moves between devices by JAX's collectives and lax.ppermute only.
A program may use at most 64 MiB of HBM per device.

```python
import math
import jax
import jax.numpy as jnp
import numpy as np
from jax import lax

C = 128
FRAMES = 4
COLS = 32
ROWS = 32
CLIPS = 16
MAXC = 32
N_SPAN = 64


def steps_of(rng, shape, shards, low, largest):
    gain = 1.0
    for dim, blocks in shards:
        draws = jax.random.uniform(jax.random.fold_in(jax.random.fold_in(rng, 6), dim), (blocks,), jnp.float32, low / len(shards), largest / len(shards))
        gain = gain * jnp.repeat(jnp.exp(draws), shape[dim] // blocks).reshape((-1,) + (1,) * (len(shape) - 1 - dim))
    return gain


def length_profile(amount, total, bound, skew):
    portions = [(1 << 20) // math.isqrt(rank ** skew) + 1 for rank in range(2, amount + 1)]
    rest, holding = total - bound - (amount - 1), [1] * (amount - 1)
    while rest > 0:
        candidates = [i for i in range(amount - 1) if holding[i] < bound]
        mass, left = sum([portions[i] for i in candidates]), rest
        for i in candidates:
            more = min(bound - holding[i], max(1, left * portions[i] // mass), rest)
            holding[i] = holding[i] + more
            rest = rest - more
    return np.array([bound] + holding)


def uneven(own_key, amount, total, reach, skew):
    if amount == 2:
        one = jax.random.randint(own_key, (), max(1, total - reach), min(reach, total - 1) + 1)
        return jnp.stack([one, total - one])
    tallies = jnp.asarray(length_profile(amount, total, reach, skew), jnp.int32)
    pairs = (amount - 1) // 2
    donor, sink = tallies[1:1 + 2 * pairs:2], tallies[2:2 + 2 * pairs:2]
    slack = jnp.minimum(donor - 1, reach - sink)
    passed = jax.random.randint(jax.random.fold_in(own_key, 1), (pairs,), 0, 1 << 20) % (slack + 1)
    tallies = tallies.at[1:1 + 2 * pairs:2].set(donor - passed).at[2:2 + 2 * pairs:2].set(sink + passed)
    return tallies[jax.random.permutation(jax.random.fold_in(own_key, 2), amount)]


def noise(stream_key, dims, width, reach, shards=(), kind=jnp.bfloat16):
    drawn = jax.random.normal(stream_key, dims, jnp.float32) * width
    if len(shards) > 0:
        drawn = steps_of(stream_key, dims, shards, -0.22, 0.18) * drawn
    return jnp.clip(drawn, min=-reach, max=reach).astype(kind)


def setup_inputs(seed: int = 0) -> dict:
    key_list = jax.random.split(jax.random.key(seed), 10)
    features = noise(key_list[0], (N_SPAN, FRAMES, ROWS, COLS, C), 1.0, 6.0, ((0, 64), (2, 4)))
    clip_lengths = uneven(key_list[1], CLIPS, N_SPAN, MAXC, 2).astype(jnp.int32)
    clip_order = jax.random.permutation(key_list[2], CLIPS).astype(jnp.int32)
    weight_a = noise(key_list[3], (3, 3, 3, C, C), (27 * C) ** -0.5, 0.109375)
    bias_a = noise(key_list[4], (C,), 0.5, 3.0, (), jnp.float32)
    weight_b = noise(key_list[5], (3, 3, 3, C, C), (27 * C) ** -0.5, 0.109375)
    bias_b = noise(key_list[6], (C,), 0.5, 3.0, (), jnp.float32)
    weight_down = noise(key_list[7], (3, 3, 3, C, C), (27 * C) ** -0.5, 0.109375)
    bias_down = noise(key_list[8], (C,), 0.5, 3.0, (), jnp.float32)
    return {"features": features, "clip_lengths": clip_lengths, "clip_order": clip_order, "weight_a": weight_a, "bias_a": bias_a, "weight_b": weight_b, "bias_b": bias_b, "weight_down": weight_down, "bias_down": bias_down}


def positions(clip_lengths, clip_order, slots):
    clips = clip_lengths.shape[0]
    pick = clip_order[:, None] == jnp.arange(clips, dtype=jnp.int32)[None, :]
    ordered = jnp.sum(jnp.where(pick, clip_lengths[None, :], 0), axis=1).astype(jnp.int32)
    ends = jnp.cumsum(ordered).astype(jnp.int32)
    starts = (ends - ordered).astype(jnp.int32)
    began = jnp.where(starts[None, :] <= slots[:, None], starts[None, :], 0)
    return (slots - jnp.max(began, axis=1)).astype(jnp.int32)


def with_context(field, keep):
    earlier = jnp.concatenate([jnp.zeros_like(field[:1, -2:]), field[:-1, -2:]], axis=0)
    earlier = earlier * keep[:, None, None, None, None]
    return jnp.concatenate([earlier, field], axis=1)


def convolve(extended, weight, stride):
    result = lax.conv_general_dilated(
        extended[None].astype(jnp.float32), weight.astype(jnp.float32),
        (stride, stride, stride), ((0, 0), (1, 1), (1, 1)),
        dimension_numbers=("NDHWC", "DHWIO", "NDHWC"),
        precision=lax.Precision.HIGHEST)
    return result[0]


def reference(features, clip_lengths, clip_order, weight_a, bias_a, weight_b, bias_b, weight_down, bias_down):
    slots = jnp.arange(features.shape[0], dtype=jnp.int32)
    position = positions(clip_lengths, clip_order, slots)
    keep = (position > 0).astype(jnp.bfloat16)
    first_in = with_context(features, keep)
    hidden = lax.map(lambda ext: jax.nn.silu(convolve(ext, weight_a, 1) + bias_a).astype(jnp.bfloat16), first_in)
    second_in = with_context(hidden, keep)

    def residual(pair):
        return (pair[0].astype(jnp.float32) + convolve(pair[1], weight_b, 1) + bias_b).astype(jnp.bfloat16)

    mixed = lax.map(residual, (features, second_in))
    third_in = with_context(mixed, keep)
    latent = lax.map(lambda ext: (convolve(ext, weight_down, 2) + bias_down).astype(jnp.bfloat16), third_in)
    slots_n, frames_n, rows_n, cols_n, chans = latent.shape
    grouped = latent.reshape(slots_n, frames_n, rows_n // 2, 2, cols_n // 2, 2, chans)
    grouped = jnp.transpose(grouped, (0, 1, 2, 4, 3, 5, 6))
    return grouped.reshape(slots_n, frames_n, rows_n // 2, cols_n // 2, 4 * chans)
```

```python
import jax
import jax.numpy as jnp
from jax import lax
from jax.sharding import PartitionSpec as P


def shifted(x, axis, by):
    peers = lax.axis_size(axis)
    pairs = [(i, i + by) for i in range(peers) if 0 <= i + by < peers]
    return lax.ppermute(x, axis, pairs)


def positions(clip_lengths, clip_order, slots):
    clips = clip_lengths.shape[0]
    pick = clip_order[:, None] == jnp.arange(clips, dtype=jnp.int32)[None, :]
    ordered = jnp.sum(jnp.where(pick, clip_lengths[None, :], 0), axis=1)
    ends = jnp.cumsum(ordered)
    starts = ends - ordered
    began = jnp.where(starts[None, :] <= slots[:, None], starts[None, :], 0)
    return slots - jnp.max(began, axis=1)


def conv_plain(padded, weight):
    chans = padded.shape[3]
    out_frames = padded.shape[0] - 2
    height = padded.shape[1] - 2
    width = padded.shape[2] - 2
    total = jnp.zeros((out_frames * height * width, weight.shape[4]), jnp.float32)
    for tap_t in range(3):
        for tap_h in range(3):
            slab = padded[tap_t : tap_t + out_frames, tap_h : tap_h + height]
            stacked = jnp.concatenate(
                [slab[:, :, tap_w : tap_w + width] for tap_w in range(3)], axis=-1
            )
            total = total + jnp.dot(
                stacked.reshape(-1, 3 * chans),
                weight[tap_t, tap_h].reshape(3 * chans, -1),
                preferred_element_type=jnp.float32,
            )
    return total.reshape(out_frames, height, width, -1)


def conv_strided(padded, weight):
    chans = padded.shape[3]
    out_frames = (padded.shape[0] - 1) // 2
    out_rows = (padded.shape[1] - 1) // 2
    out_cols = (padded.shape[2] - 1) // 2
    total = jnp.zeros((out_frames * out_rows * out_cols, weight.shape[4]), jnp.float32)
    for tap_t in range(3):
        for tap_h in range(3):
            slab = padded[
                tap_t : tap_t + 2 * out_frames - 1 : 2, tap_h : tap_h + 2 * out_rows - 1 : 2
            ]
            stacked = jnp.concatenate(
                [slab[:, :, tap_w : tap_w + 2 * out_cols - 1 : 2] for tap_w in range(3)], axis=-1
            )
            total = total + jnp.dot(
                stacked.reshape(-1, 3 * chans),
                weight[tap_t, tap_h].reshape(3 * chans, -1),
                preferred_element_type=jnp.float32,
            )
    return total.reshape(out_frames, out_rows, out_cols, -1)


def per_device(
    features, clip_lengths, clip_order, weight_a, bias_a, weight_b, bias_b, weight_down, bias_down
):
    slot = lax.axis_index("span")
    block = lax.axis_index("row")
    position = positions(clip_lengths, clip_order, jnp.stack([slot, slot - 1]))
    keep = (position > 0).astype(jnp.bfloat16)
    frames = features[0]
    height = frames.shape[1]
    near = shifted(frames, "span", 1) * keep[0]
    far = shifted(frames[2:], "span", 2) * (keep[0] * keep[1])
    field = jnp.concatenate([far, near, frames[:3]], axis=0)
    above = shifted(field[:, height - 3 :], "row", 1)
    below = shifted(field[:, :2], "row", -1)
    field = jnp.concatenate([above, field, below], axis=1)
    prior = jnp.where(jnp.arange(7) < 4, keep[0], 1).astype(jnp.bfloat16)

    def inside(first, count):
        rows = block * height + first + jnp.arange(count)
        limit = height * lax.axis_size("row")
        return ((rows >= 0) & (rows < limit)).astype(jnp.bfloat16)

    cols = ((0, 0), (0, 0), (1, 1), (0, 0))
    hidden = jax.nn.silu(conv_plain(jnp.pad(field, cols), weight_a) + bias_a).astype(jnp.bfloat16)
    hidden = hidden * (prior[:, None, None, None] * inside(-2, 11)[None, :, None, None])
    mixed = (
        field[4:, 2:11].astype(jnp.float32) + conv_plain(jnp.pad(hidden, cols), weight_b) + bias_b
    ).astype(jnp.bfloat16)
    mixed = mixed * (prior[2:, None, None, None] * inside(-1, 9)[None, :, None, None])
    padded = jnp.pad(mixed, ((0, 0), (0, 0), (1, 0), (0, 0)))
    latent = (conv_strided(padded, weight_down) + bias_down).astype(jnp.bfloat16)
    frames_n, rows_n, cols_n, chans = latent.shape
    grouped = latent.reshape(frames_n, rows_n // 2, 2, cols_n // 2, 2, chans)
    grouped = jnp.transpose(grouped, (0, 1, 3, 2, 4, 5))
    return grouped.reshape(1, frames_n, rows_n // 2, cols_n // 2, 4 * chans)


def solution(mesh):
    placed = (P("span", None, "row", None, None), P(), P(), P(), P(), P(), P(), P(), P())
    return jax.shard_map(
        per_device,
        mesh=mesh,
        in_specs=placed,
        out_specs=P("span", None, "row", None, None),
        check_vma=False,
    )
```

```python
import jax
import jax.numpy as jnp
from jax import lax
from jax.experimental import pallas as pl
from jax.experimental.pallas import tpu as pltpu
from jax.sharding import PartitionSpec as P

BF = jnp.bfloat16
F32 = jnp.float32
C = 128
VMEM = pl.BlockSpec(memory_space=pltpu.VMEM)
SMEM = pl.BlockSpec(memory_space=pltpu.SMEM)


def shifted(x, axis, by):
    peers = lax.axis_size(axis)
    pairs = [(i, i + by) for i in range(peers) if 0 <= i + by < peers]
    return lax.ppermute(x, axis, pairs)


def continues(lengths, order, slot):
    begin = jnp.int32(0)
    first = jnp.int32(0)
    for k in range(order.shape[0]):
        first = jnp.where(begin == slot, jnp.int32(1), first)
        begin = begin + lengths[order[k]]
    return 1 - first


def pack_weights(a, b, pa, pb):
    for src, dst in ((a, pa), (b, pb)):
        for t in range(3):
            for i in range(4):
                for w in range(3):
                    for j in range(2):
                        k = i - j
                        value = src[t * 9 + k * 3 + w] if 0 <= k <= 2 else jnp.zeros((C, C), BF)
                        dst[pl.ds((t * 4 + i) * C, C), pl.ds((w * 2 + j) * C, C)] = value


def pack_halo(own, near, up, down):
    for f in range(4):
        up[f] = near[f, 5:8]
        down[f] = near[f, 0:2]
        up[4 + f] = own[f, 5:8]
        down[4 + f] = own[f, 0:2]


def feature_row(own, near, above, below, frame, row):
    f = frame + 4
    if row < 0:
        return above[f, row + 3]
    if row < 8:
        return near[f, row] if f < 4 else own[f - 4, row]
    if row < 10:
        return below[f, row - 8]
    return jnp.zeros((32, C), BF)


def fill_pairs(dst, at, refs, frame, scale):
    for pair in range(7):
        for half in range(2):
            value = feature_row(*refs, frame, 2 * pair + half - 3)
            if scale is not None:
                value = value * scale
            dst[at, pair, :, half * C : half * C + C] = value


def conv_pairs(src, first, pairs, weight):
    rows = pairs * 32
    lhs = jnp.concatenate(
        [src[first + t, h : h + pairs].reshape(rows, 2 * C) for t in range(3) for h in range(2)],
        axis=1,
    )
    y = jnp.dot(lhs, weight[...], preferred_element_type=F32)
    col = lax.broadcasted_iota(jnp.int32, (rows, 2 * C), 0) % 32
    left = jnp.where(col == 0, 0.0, pltpu.roll(y[:, : 2 * C], 1, 0))
    right = jnp.where(col == 31, 0.0, pltpu.roll(y[:, 4 * C :], rows - 1, 0))
    return (y[:, 2 * C : 4 * C] + left + right).reshape(pairs, 32, 2 * C)


def hidden_frame(dst, at, src, first, weight, bias, top, bottom, scale):
    v = conv_pairs(src, first, 6, weight) + bias
    v = v / (1.0 + jnp.exp(-v))
    if scale is not None:
        v = v * scale
    v = v.astype(BF)
    dst[at, 0] = v[0] * top
    dst[at, 1:5] = v[1:5]
    dst[at, 5] = v[5] * bottom


def mixed_frame(dst, at, src, first, weight, bias, residual, top):
    v = residual.astype(F32) + conv_pairs(src, first, 5, weight) + bias
    v = v.astype(BF).astype(F32)
    for pair in range(5):
        dst[at, 2 * pair] = v[pair, :, :C] * top if pair == 0 else v[pair, :, :C]
        dst[at, 2 * pair + 1] = v[pair, :, C:]


def strided_taps(mixed, at):
    taps = []
    zero_first = lax.broadcasted_iota(jnp.int32, (8, C), 0) == 0
    for r in range(9):
        m = [mixed[at, r, pl.ds(k, 8, stride=4), :] for k in range(4)]
        before = jnp.where(zero_first, 0.0, pltpu.roll(m[3], 1, 0))
        taps.append(
            jnp.concatenate(
                [
                    jnp.concatenate(pair, axis=0).astype(BF)
                    for pair in ((before, m[1]), (m[0], m[2]), (m[1], m[3]))
                ],
                axis=1,
            )
        )
    return jnp.concatenate(
        [jnp.concatenate([taps[2 * j + k] for k in range(3)], axis=1) for j in range(4)], axis=0
    )


def down_dot(taps, weight, t):
    return jnp.dot(taps, weight[pl.ds(t * 9 * C, 9 * C), :], preferred_element_type=F32)


def forward_part(
    lengths, order, own, near, above, below, wa, ba, wb, bb, wd, part, late, kept, x, h, m
):
    slot = lax.axis_index("span")
    block = lax.axis_index("row")
    keep = continues(lengths, order, slot).astype(F32).astype(BF)
    top = (block > 0).astype(F32)
    bottom = (block < lax.axis_size("row") - 1).astype(F32).astype(BF)
    refs = (own, near, above, below)
    for i in range(6):
        fill_pairs(x, i, refs, i - 2, keep if i < 2 else None)
    bias = jnp.concatenate([ba[...], ba[...]], axis=1)
    for i in range(4):
        hidden_frame(h, i, x, i, wa, bias, top.astype(BF), bottom, None)
    kept[...] = h[0:2]
    bias = jnp.concatenate([bb[...], bb[...]], axis=1)
    for i in range(2):
        mixed_frame(m, i, h, i, wb, bias, x[4 + i, 1:6], top)
    taps = strided_taps(m, 0)
    part[...] = down_dot(taps, wd, 0) + down_dot(strided_taps(m, 1), wd, 1)
    late[...] = down_dot(taps, wd, 2)


def context_part(
    lengths, order, own, near, above, below, wa, ba, wb, bb, wd, late, kept, early, out, x, h, m
):
    slot = lax.axis_index("span")
    block = lax.axis_index("row")
    keep = continues(lengths, order, slot).astype(F32)
    top = (block > 0).astype(F32)
    bottom = (block < lax.axis_size("row") - 1).astype(F32).astype(BF)
    refs = (own, near, above, below)
    for i in range(6):
        fill_pairs(x, i, refs, i - 4, None)
    bias = jnp.concatenate([ba[...], ba[...]], axis=1)
    for i in range(2):
        hidden_frame(h, i, x, i, wa, bias, top.astype(BF), bottom, keep)
    h[2:4] = kept[...]
    bias = jnp.concatenate([bb[...], bb[...]], axis=1)
    for i in range(2):
        mixed_frame(m, i, h, i, wb, bias, x[4 + i, 1:6], top)
    taps = strided_taps(m, 0)
    early[...] = down_dot(taps, wd, 2)
    out[...] = late[...] + down_dot(taps, wd, 0) + down_dot(strided_taps(m, 1), wd, 1)


def finish(lengths, order, early, late, part, bd, out):
    keep = continues(lengths, order, lax.axis_index("span")).astype(F32)
    for t in range(2):
        v = early[...] + part[...] * keep if t == 0 else late[...]
        v = (v + bd[...]).astype(BF)
        for i in range(2):
            out[t, i] = jnp.concatenate(
                [v[(2 * i + a) * 16 + b * 8 : (2 * i + a) * 16 + b * 8 + 8] for a in range(2) for b in range(2)],
                axis=1,
            )


def kernel(body, name, outs, ins, scratch=(), flops=0):
    return pl.pallas_call(
        body,
        name=name,
        out_shape=[jax.ShapeDtypeStruct(*o) for o in outs],
        in_specs=ins,
        out_specs=[VMEM] * len(outs),
        scratch_shapes=list(scratch),
        compiler_params=pltpu.CompilerParams(vmem_limit_bytes=24 << 20),
        cost_estimate=pl.CostEstimate(flops=flops, bytes_accessed=1 << 20, transcendentals=0),
    )


def per_device(
    features, clip_lengths, clip_order, weight_a, bias_a, weight_b, bias_b, weight_down, bias_down
):
    own = features[0]
    near = shifted(own, "span", 1)
    packed = kernel(pack_weights, "pack_weights", [((12 * C, 6 * C), BF)] * 2, [VMEM] * 2, flops=1 << 30)
    wa, wb = packed(weight_a.reshape(27, C, C), weight_b.reshape(27, C, C))
    wd = weight_down.reshape(27 * C, C)
    ba, bb, bd = (b.reshape(1, C) for b in (bias_a, bias_b, bias_down))
    up, down = kernel(
        pack_halo, "pack_halo", [((8, 3, 32, C), BF), ((8, 2, 32, C), BF)], [VMEM] * 2
    )(own, near)
    above = shifted(up, "row", 1)
    below = shifted(down, "row", -1)
    scratch = [
        pltpu.VMEM((6, 7, 32, 2 * C), BF),
        pltpu.VMEM((4, 6, 32, 2 * C), BF),
        pltpu.VMEM((2, 10, 32, C), F32),
    ]
    common = (clip_lengths, clip_order, own, near, above, below, wa, ba, wb, bb, wd)
    latent = ((64, C), F32)
    part, late, kept = kernel(
        forward_part,
        "forward_part",
        [latent, latent, ((2, 6, 32, 2 * C), BF)],
        [SMEM] * 2 + [VMEM] * 9,
        scratch,
        flops=3 << 30,
    )(*common)
    part = shifted(part, "span", 1)
    early, late = kernel(
        context_part,
        "context_part",
        [latent, latent],
        [SMEM] * 2 + [VMEM] * 11,
        scratch,
        flops=2 << 30,
    )(*common, late, kept)
    (out,) = kernel(
        finish, "finish", [((2, 2, 8, 4 * C), BF)], [SMEM] * 2 + [VMEM] * 4
    )(clip_lengths, clip_order, early, late, part, bd)
    return out[None]


def solution(mesh):
    placed = (P("span", None, "row", None, None), P(), P(), P(), P(), P(), P(), P(), P())
    return jax.shard_map(
        per_device,
        mesh=mesh,
        in_specs=placed,
        out_specs=P("span", None, "row", None, None),
        check_vma=False,
    )
```

```python
import jax
import jax.numpy as jnp
from jax import lax
from jax.experimental import pallas as pl
from jax.experimental.pallas import tpu as pltpu
from jax.sharding import PartitionSpec as P

BF = jnp.bfloat16
F32 = jnp.float32
C = 128
VMEM = pl.BlockSpec(memory_space=pltpu.VMEM)
SMEM = pl.BlockSpec(memory_space=pltpu.SMEM)

EDGE_Q = (0, 1, 5)
EDGE_P = (0, 1, 4)


def shifted(x, axis, by):
    peers = lax.axis_size(axis)
    pairs = [(i, i + by) for i in range(peers) if 0 <= i + by < peers]
    return lax.ppermute(x, axis, pairs)


def continues(lengths, order, slot):
    begin = jnp.int32(0)
    first = jnp.int32(0)
    for k in range(order.shape[0]):
        first = jnp.where(begin == slot, jnp.int32(1), first)
        begin = begin + lengths[order[k]]
    return 1 - first


def prepare(lengths, order, own, a, b, pa, pb, pairs, flags):
    slot = lax.axis_index("span")
    block = lax.axis_index("row")
    values = (
        continues(lengths, order, slot),
        continues(lengths, order, slot + 1),
        (block > 0).astype(jnp.int32),
        (block < lax.axis_size("row") - 1).astype(jnp.int32),
    )
    for i, value in enumerate(values):
        flags[i] = jnp.full((8, C), value.astype(F32), F32)
    for src, dst in ((a, pa), (b, pb)):
        for t in range(3):
            for i in range(4):
                for w in range(3):
                    for j in range(2):
                        k = i - j
                        value = src[t * 9 + k * 3 + w] if 0 <= k <= 2 else jnp.zeros((C, C), BF)
                        dst[pl.ds((t * 4 + i) * C, C), pl.ds((w * 2 + j) * C, C)] = value
    for f in range(4):
        for row in range(8):
            pairs[f, row // 2, :, pl.ds(row % 2 * C, C)] = own[f, row]


def pack_halo(near, own, flags, up, down, pairs):
    keep = flags[0, 0:1, :].astype(BF)
    for f in range(4):
        for row in range(8):
            value = near[f, row] * keep
            pairs[f, row // 2, :, pl.ds(row % 2 * C, C)] = value
            if row >= 5:
                up[f, row - 5] = value
                up[4 + f, row - 5] = own[f, row // 2 , :, pl.ds(row % 2 * C, C)]
            if row < 2:
                down[f, row] = value
                down[4 + f, row] = own[f, row // 2, :, pl.ds(row % 2 * C, C)]


def twice(bias):
    return jnp.concatenate([bias[...], bias[...]], axis=1)


def conv(blocks, fetch, weight):
    rows = len(blocks) * 32
    lhs = jnp.concatenate(
        [
            jnp.concatenate([fetch(f - 2 + t, q + h) for f, q in blocks], axis=0)
            for t in range(3)
            for h in range(2)
        ],
        axis=1,
    )
    y = jnp.dot(lhs, weight[...], preferred_element_type=F32)
    col = lax.broadcasted_iota(jnp.int32, (rows, 2 * C), 0) % 32
    left = jnp.where(col == 0, 0.0, pltpu.roll(y[:, : 2 * C], 1, 0))
    right = jnp.where(col == 31, 0.0, pltpu.roll(y[:, 4 * C :], rows - 1, 0))
    return y[:, 2 * C : 4 * C] + left + right


def hidden_blocks(blocks, fetch, weight, bias, flags, put):
    v = conv(blocks, fetch, weight) + bias
    v = v / (1.0 + jnp.exp(-v))
    keep, top, bottom = (flags[i, 0:1, :] for i in (0, 2, 3))
    one = jnp.ones_like(top)
    for i, (f, q) in enumerate(blocks):
        value = v[i * 32 : i * 32 + 32]
        if q == 0:
            value = value * jnp.concatenate([top, top], axis=1)
        elif q == 1:
            value = value * jnp.concatenate([top, one], axis=1)
        elif q == 5:
            value = value * jnp.concatenate([one, bottom], axis=1)
        if f < 0:
            value = value * jnp.concatenate([keep, keep], axis=1)
        put(f, q, value.astype(BF))


def mixed_blocks(blocks, fetch, residual, weight, bias, top, put):
    v = conv(blocks, fetch, weight) + bias
    for i, (f, p) in enumerate(blocks):
        value = residual(f, p + 1).astype(F32) + v[i * 32 : i * 32 + 32]
        value = value.astype(BF).astype(F32)
        if p == 0:
            put(f, 0, value[:, C:] * top)
        else:
            put(f, 2 * p - 1, value[:, :C])
            put(f, 2 * p, value[:, C:])


def column_taps(row):
    m = [row[pl.ds(k, 8, stride=4), :] for k in range(4)]
    first = lax.broadcasted_iota(jnp.int32, (8, C), 0) == 0
    before = jnp.where(first, 0.0, pltpu.roll(m[3], 1, 0))
    columns = ((before, m[1]), (m[0], m[2]), (m[1], m[3]))
    return jnp.concatenate([jnp.concatenate(pair, axis=0).astype(BF) for pair in columns], axis=1)


def inner_part(near, own, wa, ba, wb, bb, flags, hidden, taps, m):
    def feature(f, g):
        return near[f + 4, g - 2] if f < 0 else own[f, g - 2]

    def put_hidden(f, q, value):
        hidden[f + 2, q - 2] = value

    def put_mixed(f, r, value):
        m[f, r - 3] = value

    for pair in range(3):
        frames = (2 * pair - 2, 2 * pair - 1)
        hidden_blocks([(f, q) for f in frames for q in (2, 3, 4)], feature, wa, twice(ba), flags, put_hidden)
    mixed_blocks(
        [(f, p) for f in range(4) for p in (2, 3)],
        lambda f, q: hidden[f + 2, q - 2],
        feature,
        wb,
        twice(bb),
        None,
        put_mixed,
    )
    for f in range(4):
        for r in range(4):
            taps[f, r] = column_taps(m.at[f, r])


def edge_part(frames, hidden_frames, near, own, above, below, wa, ba, wb, bb, flags, inner, taps, x, h, m, kept):
    for f in range(min(hidden_frames) - 2, max(frames) + 1):
        i = f + 4
        x[i, 0, :, :C] = jnp.zeros((32, C), BF)
        x[i, 0, :, C:] = above[i, 0]
        x[i, 1, :, :C] = above[i, 1]
        x[i, 1, :, C:] = above[i, 2]
        x[i, 2, :, :C] = below[i, 0]
        x[i, 2, :, C:] = below[i, 1]

    def feature(f, g):
        if 2 <= g <= 5:
            return near[f + 4, g - 2] if f < 0 else own[f, g - 2]
        return x[f + 4, 2 if g == 6 else g]

    def put_hidden(f, q, value):
        h[f + 2, EDGE_Q.index(q)] = value

    def hidden(f, q):
        if 2 <= q <= 4:
            return inner[f + 2, q - 2]
        e = EDGE_Q.index(q)
        return h[f + 2, e] if f in hidden_frames else kept[f, e]

    def put_mixed(f, r, value):
        m[f % 2, r if r < 3 else r - 4] = value

    for pair in range(0, len(hidden_frames), 2):
        blocks = [(f, q) for f in hidden_frames[pair : pair + 2] for q in EDGE_Q]
        hidden_blocks(blocks, feature, wa, twice(ba), flags, put_hidden)
    top = flags[2, 0:1, :]
    mixed_blocks([(f, p) for f in frames for p in EDGE_P], hidden, feature, wb, twice(bb), top, put_mixed)
    lhs = []
    for f in frames:
        rows = [column_taps(m.at[f % 2, r]) for r in range(3)]
        rows += [taps[f, r] for r in range(4)]
        rows += [column_taps(m.at[f % 2, r]) for r in range(3, 5)]
        lhs.append(
            jnp.concatenate(
                [jnp.concatenate([rows[2 * j + k] for k in range(3)], axis=1) for j in range(4)], axis=0
            )
        )
    return lhs


def down_dots(lhs, wd):
    n = 9 * C
    both = jnp.concatenate([wd[pl.ds(0, n), :], wd[pl.ds(2 * n, n), :]], axis=1)
    y = jnp.dot(lhs[0], both, preferred_element_type=F32)
    z = jnp.dot(lhs[1], wd[pl.ds(n, n), :], preferred_element_type=F32)
    return y[:, :C] + z, y[:, C:]


def tokens(v):
    return [
        jnp.concatenate(
            [v[(2 * i + a) * 16 + b * 8 : (2 * i + a) * 16 + b * 8 + 8] for a in range(2) for b in range(2)],
            axis=1,
        )
        for i in range(2)
    ]


def forward_part(
    near, own, above, below, wa, ba, wb, bb, wd, flags, inner, taps, part, late, kept, x, h, m
):
    lhs = edge_part(
        (2, 3), (0, 1, 2, 3), near, own, above, below, wa, ba, wb, bb, flags, inner, taps, x, h, m, None
    )
    for f in range(2):
        kept[f] = h[2 + f]
    first, last = down_dots(lhs, wd)
    for i, value in enumerate(tokens(first * flags[1, 0:1, :])):
        part[i] = value
    late[...] = last


def context_part(
    near, own, above, below, wa, ba, wb, bb, wd, bd, flags, inner, taps, late, kept, early, out, x, h, m
):
    lhs = edge_part(
        (0, 1), (-2, -1), near, own, above, below, wa, ba, wb, bb, flags, inner, taps, x, h, m, kept
    )
    first, last = down_dots(lhs, wd)
    for i, value in enumerate(tokens(last + bd[...])):
        early[i] = value
    for i, value in enumerate(tokens(late[...] + first + bd[...])):
        out[i] = value.astype(BF)


def kernel(body, outs, ins, scratch=(), flops=0):
    return pl.pallas_call(
        body,
        name=body.__name__,
        out_shape=[jax.ShapeDtypeStruct(*o) for o in outs],
        in_specs=ins,
        out_specs=[VMEM] * len(outs),
        scratch_shapes=list(scratch),
        compiler_params=pltpu.CompilerParams(vmem_limit_bytes=24 << 20),
        cost_estimate=pl.CostEstimate(flops=flops, bytes_accessed=1 << 20, transcendentals=0),
    )


def per_device(
    features, clip_lengths, clip_order, weight_a, bias_a, weight_b, bias_b, weight_down, bias_down
):
    wd = weight_down.reshape(27 * C, C)
    ba, bb, bd = (b.reshape(1, C) for b in (bias_a, bias_b, bias_down))
    near = shifted(features[0], "span", 1)
    packed = ((12 * C, 6 * C), BF)
    paired = ((4, 4, 32, 2 * C), BF)
    wa, wb, own, flags = kernel(
        prepare, [packed, packed, paired, ((4, 8, C), F32)], [SMEM] * 2 + [VMEM] * 3, flops=1 << 30
    )(clip_lengths, clip_order, features[0], weight_a.reshape(27, C, C), weight_b.reshape(27, C, C))
    up, down, near = kernel(
        pack_halo, [((8, 3, 32, C), BF), ((8, 2, 32, C), BF), paired], [VMEM] * 3
    )(near, own, flags)
    above = shifted(up, "row", 1)
    below = shifted(down, "row", -1)
    inner, taps = kernel(
        inner_part,
        [((6, 3, 32, 2 * C), BF), ((4, 4, 16, 3 * C), BF)],
        [VMEM] * 7,
        [pltpu.VMEM((4, 4, 32, C), F32)],
        flops=2 << 30,
    )(near, own, wa, ba, wb, bb, flags)
    scratch = [
        pltpu.VMEM((8, 3, 32, 2 * C), BF),
        pltpu.VMEM((6, 3, 32, 2 * C), BF),
        pltpu.VMEM((2, 5, 32, C), F32),
    ]
    token = ((2, 8, 4 * C), F32)
    part, late, kept = kernel(
        forward_part,
        [token, ((64, C), F32), ((2, 3, 32, 2 * C), BF)],
        [VMEM] * 12,
        scratch,
        flops=2 << 30,
    )(near, own, above, below, wa, ba, wb, bb, wd, flags, inner, taps)
    part = shifted(part, "span", 1)
    early, late = kernel(
        context_part, [token, (token[0], BF)], [VMEM] * 15, scratch, flops=2 << 30
    )(near, own, above, below, wa, ba, wb, bb, wd, bd, flags, inner, taps, late, kept)
    return jnp.stack([(early + part).astype(BF), late])[None]


def solution(mesh):
    placed = (P("span", None, "row", None, None), P(), P(), P(), P(), P(), P(), P(), P())
    return jax.shard_map(
        per_device,
        mesh=mesh,
        in_specs=placed,
        out_specs=P("span", None, "row", None, None),
        check_vma=False,
    )
```

```python
import jax
import jax.numpy as jnp
from jax import lax
from jax.experimental import pallas as pl
from jax.experimental.pallas import tpu as pltpu
from jax.sharding import PartitionSpec as P

BF = jnp.bfloat16
F32 = jnp.float32
C = 128
VMEM = pl.BlockSpec(memory_space=pltpu.VMEM)
HBM = pl.BlockSpec(memory_space=pltpu.HBM)


def shifted(x, axis, by):
    peers = lax.axis_size(axis)
    pairs = [(i, i + by) for i in range(peers) if 0 <= i + by < peers]
    return lax.ppermute(x, axis, pairs)


def continues(lengths, order, slot):
    begin = jnp.int32(0)
    first = jnp.int32(0)
    for k in range(16):
        first = jnp.where(begin == slot, jnp.int32(1), first)
        begin = begin + lengths[order[k]]
    return 1 - first


def last_frames(features, out, sem):
    copy = pltpu.make_async_copy(features.at[pl.ds(2, 2)], out, sem)
    copy.start()
    copy.wait()


def prepare(lengths, order, features, a, b, pa, pb, pairs, flags, smem, own, taps, sem):
    copies = [
        pltpu.make_async_copy(lengths, smem.at[0], sem.at[0]),
        pltpu.make_async_copy(order, smem.at[1], sem.at[1]),
        pltpu.make_async_copy(features.at[pl.ds(0, 3)], own, sem.at[2]),
    ]
    for i, src in enumerate((a, b)):
        for t in range(3):
            part = pl.ds(9 * t, 9)
            copies.append(pltpu.make_async_copy(src.at[part], taps.at[i, part], sem.at[3 + 3 * i + t]))
    for copy in copies:
        copy.start()
    for copy in copies[:3]:
        copy.wait()
    slot = lax.axis_index("span")
    block = lax.axis_index("row")
    values = (
        continues(smem.at[0], smem.at[1], slot),
        continues(smem.at[0], smem.at[1], slot - 1),
        (block > 0).astype(jnp.int32),
        (block < lax.axis_size("row") - 1).astype(jnp.int32),
    )
    for i, value in enumerate(values):
        flags[i] = jnp.full((8, C), value.astype(F32), F32)
    for f in range(3):
        for row in range(8):
            pairs[f, row // 2, :, pl.ds(row % 2 * C, C)] = own[f, row]
    for n, dst in enumerate((pa, pb)):
        for t in range(3):
            copies[3 + 3 * n + t].wait()
            for i in range(4):
                for w in range(3):
                    for j in range(2):
                        k = i - j
                        value = taps[n, t * 9 + k * 3 + w] if 0 <= k <= 2 else jnp.zeros((C, C), BF)
                        dst[pl.ds((t * 4 + i) * C, C), pl.ds((w * 2 + j) * C, C)] = value


def pack_up(far, near, own, flags, after, up, pairs):
    both = (flags[0, 0:1, :] * flags[1, 0:1, :]).astype(BF)
    for f in range(2):
        for row in range(8):
            value = far[f, row] * both
            pairs[f, row // 2, :, pl.ds(row % 2 * C, C)] = value
            if row >= 5:
                up[f, row - 5] = value
    for f in range(7):
        for row in range(5, 8):
            lanes = pl.ds(row % 2 * C, C)
            up[2 + f, row - 5] = near[f, row // 2, :, lanes] if f < 4 else own[f - 4, row // 2, :, lanes]


def pack_down(far, near, own, after, down):
    for f in range(9):
        for row in range(2):
            src, at = (far, f) if f < 2 else (near, f - 2) if f < 6 else (own, f - 6)
            down[f, row] = src[at, 0, :, pl.ds(row * C, C)]


def twice(bias):
    return jnp.concatenate([bias[...], bias[...]], axis=1)


def conv(blocks, fetch, weight):
    rows = len(blocks) * 32
    lhs = jnp.concatenate(
        [
            jnp.concatenate([fetch(f - 2 + t, q + h) for f, q in blocks], axis=0)
            for t in range(3)
            for h in range(2)
        ],
        axis=1,
    )
    y = jnp.dot(lhs, weight[...], preferred_element_type=F32)
    col = lax.broadcasted_iota(jnp.int32, (rows, 2 * C), 0) % 32
    left = jnp.where(col == 0, 0.0, pltpu.roll(y[:, : 2 * C], 1, 0))
    right = jnp.where(col == 31, 0.0, pltpu.roll(y[:, 4 * C :], rows - 1, 0))
    return y[:, 2 * C : 4 * C] + left + right


def hidden_blocks(blocks, fetch, weight, bias, flags, put):
    v = conv(blocks, fetch, weight) + bias
    v = v / (1.0 + jnp.exp(-v))
    keep, top, bottom = (flags[i, 0:1, :] for i in (0, 2, 3))
    one = jnp.ones_like(top)
    for i, (f, q) in enumerate(blocks):
        value = v[i * 32 : i * 32 + 32]
        if q == 0:
            value = value * jnp.concatenate([top, top], axis=1)
        elif q == 1:
            value = value * jnp.concatenate([top, one], axis=1)
        elif q == 5:
            value = value * jnp.concatenate([one, bottom], axis=1)
        if f < 0:
            value = value * jnp.concatenate([keep, keep], axis=1)
        put(f, q, value.astype(BF))


def mixed_blocks(blocks, fetch, residual, weight, bias, flags, put):
    v = conv(blocks, fetch, weight) + bias
    keep, top = flags[0, 0:1, :], flags[2, 0:1, :]
    for i, (f, p) in enumerate(blocks):
        value = residual(f, p + 1).astype(F32) + v[i * 32 : i * 32 + 32]
        value = value.astype(BF).astype(F32)
        if f < 0:
            value = value * jnp.concatenate([keep, keep], axis=1)
        if p == 0:
            put(f, 0, value[:, C:] * top)
        else:
            put(f, 2 * p - 1, value[:, :C])
            put(f, 2 * p, value[:, C:])


def column_taps(row):
    m = [row[pl.ds(k, 8, stride=4), :] for k in range(4)]
    first = lax.broadcasted_iota(jnp.int32, (8, C), 0) == 0
    before = jnp.where(first, 0.0, pltpu.roll(m[3], 1, 0))
    columns = ((before, m[1]), (m[0], m[2]), (m[1], m[3]))
    return jnp.concatenate([jnp.concatenate(pair, axis=0).astype(BF) for pair in columns], axis=1)


def own_feature(far, near, own):
    def feature(f, g):
        src, at = (far, f + 6) if f < -4 else (near, f + 4) if f < 0 else (own, f)
        return src[at, g - 2]

    return feature


def inner_near(arrived, own, wa, ba, wb, bb, flags, near, hidden, taps, m):
    keep = flags[0, 0:1, :].astype(BF)
    for f in range(4):
        for row in range(8):
            near[f, row // 2, :, pl.ds(row % 2 * C, C)] = arrived[f, row] * keep
    feature = own_feature(None, near, own)

    def put_hidden(f, q, value):
        hidden[f + 2, q - 2] = value

    def put_mixed(f, r, value):
        m[f, r - 3] = value

    for frames in ((-2, -1), (0, 1, 2)):
        hidden_blocks([(f, q) for f in frames for q in (2, 3, 4)], feature, wa, twice(ba), flags, put_hidden)
    blocks = [(f, p) for f in range(3) for p in (2, 3)]
    mixed_blocks(blocks, lambda f, q: hidden[f + 2, q - 2], feature, wb, twice(bb), flags, put_mixed)
    for f in range(3):
        for r in range(4):
            taps[f, r] = column_taps(m.at[f, r])


def inner_far(far, near, wa, ba, flags, hidden):
    def put_hidden(f, q, value):
        hidden[f + 4, q - 2] = value

    blocks = [(f, q) for f in (-4, -3) for q in (2, 3, 4)]
    hidden_blocks(blocks, own_feature(far, near, None), wa, twice(ba), flags, put_hidden)


def inner_mixed(near, wb, bb, flags, hidden_far, hidden_near, taps, m):
    def hidden(f, q):
        return hidden_far[f + 4, q - 2] if f < -2 else hidden_near[f + 2, q - 2]

    def put_mixed(f, r, value):
        m[f + 2, r - 3] = value

    blocks = [(f, p) for f in (-2, -1) for p in (2, 3)]
    mixed_blocks(blocks, hidden, own_feature(None, near, None), wb, twice(bb), flags, put_mixed)
    for f in range(2):
        for r in range(4):
            taps[f, r] = column_taps(m.at[f, r])


def edge(far, near, own, wa, ba, wb, bb, flags, hidden_far, hidden_near, h, m, halo, q_edge, p_edge, row):
    def feature(f, g):
        return own_feature(far, near, own)(f, g) if 2 <= g <= 5 else halo(f + 6, g)

    def put_hidden(f, q, value):
        h[f + 4, q_edge.index(q)] = value

    def hidden(f, q):
        if 2 <= q <= 4:
            return hidden_far[f + 4, q - 2] if f < -2 else hidden_near[f + 2, q - 2]
        return h[f + 4, q_edge.index(q)]

    def put_mixed(f, r, value):
        m[f + 2, r - row] = value

    split = ((-4, -3, -2), (-1, 0, 1, 2)) if len(q_edge) > 1 else (range(-4, 3),)
    for frames in split:
        hidden_blocks([(f, q) for f in frames for q in q_edge], feature, wa, twice(ba), flags, put_hidden)
    mixed_blocks([(f, p) for f in range(-2, 3) for p in p_edge], hidden, feature, wb, twice(bb), flags, put_mixed)


def top_part(far, near, own, above, wa, ba, wb, bb, flags, hidden_far, hidden_near, taps, h, m):
    def halo(i, g):
        upper = jnp.zeros((32, C), BF) if g == 0 else above[i, 1]
        return jnp.concatenate([upper, above[i, 2 * g]], axis=1)

    edge(far, near, own, wa, ba, wb, bb, flags, hidden_far, hidden_near, h, m, halo, (0, 1), (0, 1), 0)
    for f in range(5):
        for r in range(3):
            taps[f, r] = column_taps(m.at[f, r])


def bottom_part(
    far, near, own, below, wa, ba, wb, bb, wd, bd, flags, hidden_far, hidden_near, top_taps, taps_far, taps_near, out, h, m
):
    def halo(i, g):
        return jnp.concatenate([below[i, 0], below[i, 1]], axis=1)

    edge(far, near, own, wa, ba, wb, bb, flags, hidden_far, hidden_near, h, m, halo, (5,), (4,), 7)
    frames = []
    for f in range(5):
        rows = [top_taps[f, r] for r in range(3)] + [taps_far[f, r] if f < 2 else taps_near[f - 2, r] for r in range(4)]
        rows += [column_taps(m.at[f, r]) for r in range(2)]
        frames.append(
            jnp.concatenate(
                [jnp.concatenate([rows[2 * j + k] for k in range(3)], axis=1) for j in range(4)], axis=0
            )
        )
    lhs = jnp.concatenate([jnp.concatenate(frames[t : t + 3], axis=1) for t in (0, 2)], axis=0)
    v = jnp.dot(lhs, wd[...], preferred_element_type=F32) + bd[...]
    v = v.astype(BF).astype(F32)
    for t in range(2):
        for i in range(2):
            at = t * 64 + i * 32
            out[t, i] = jnp.concatenate([v[at + k * 8 : at + k * 8 + 8] for k in range(4)], axis=1).astype(BF)


def kernel(body, outs, ins, scratch=(), flops=0):
    return pl.pallas_call(
        body,
        name=body.__name__,
        out_shape=[jax.ShapeDtypeStruct(*o) for o in outs],
        in_specs=ins,
        out_specs=[VMEM] * len(outs),
        scratch_shapes=list(scratch),
        compiler_params=pltpu.CompilerParams(vmem_limit_bytes=24 << 20),
        cost_estimate=pl.CostEstimate(flops=flops, bytes_accessed=1 << 10, transcendentals=0),
    )


def per_device(
    features, clip_lengths, clip_order, weight_a, bias_a, weight_b, bias_b, weight_down, bias_down
):
    wd = weight_down.reshape(27 * C, C)
    ba, bb, bd = (b.reshape(1, C) for b in (bias_a, bias_b, bias_down))
    near = shifted(features[0], "span", 1)
    taps_a, taps_b = (w.reshape(27, C, C) for w in (weight_a, weight_b))
    stay = [
        pltpu.with_memory_space_constraint(x, pltpu.HBM)
        for x in (clip_lengths, clip_order, features[0], taps_a, taps_b)
    ]
    (tail,) = kernel(
        last_frames,
        [((2, 8, 32, C), BF)],
        [HBM],
        [pltpu.SemaphoreType.DMA],
    )(stay[2])
    far = shifted(tail, "span", 2)
    packed = ((12 * C, 6 * C), BF)
    wa, wb, own, flags = kernel(
        prepare,
        [packed, packed, ((3, 4, 32, 2 * C), BF), ((4, 8, C), F32)],
        [HBM] * 5,
        [
            pltpu.SMEM((2, 16), jnp.int32),
            pltpu.VMEM((3, 8, 32, C), BF),
            pltpu.VMEM((2, 27, C, C), BF),
            pltpu.SemaphoreType.DMA((9,)),
        ],
    )(*stay)
    near, hidden_near, taps_near = kernel(
        inner_near,
        [((4, 4, 32, 2 * C), BF), ((5, 3, 32, 2 * C), BF), ((3, 4, 16, 3 * C), BF)],
        [VMEM] * 7,
        [pltpu.VMEM((3, 4, 32, C), F32)],
    )(near, own, wa, ba, wb, bb, flags)
    up, far = kernel(
        pack_up, [((9, 3, 32, C), BF), ((2, 4, 32, 2 * C), BF)], [VMEM] * 5
    )(far, near, own, flags, taps_near)
    above = shifted(up, "row", 1)
    (hidden_far,) = kernel(inner_far, [((2, 3, 32, 2 * C), BF)], [VMEM] * 5)(far, near, wa, ba, flags)
    (down,) = kernel(pack_down, [((9, 2, 32, C), BF)], [VMEM] * 4)(far, near, own, hidden_far)
    below = shifted(down, "row", -1)
    (taps_far,) = kernel(
        inner_mixed, [((2, 4, 16, 3 * C), BF)], [VMEM] * 6, [pltpu.VMEM((2, 4, 32, C), F32)]
    )(near, wb, bb, flags, hidden_far, hidden_near)
    (top_taps,) = kernel(
        top_part,
        [((5, 3, 16, 3 * C), BF)],
        [VMEM] * 11,
        [pltpu.VMEM((7, 2, 32, 2 * C), BF), pltpu.VMEM((5, 3, 32, C), F32)],
    )(far, near, own, above, wa, ba, wb, bb, flags, hidden_far, hidden_near)
    (out,) = kernel(
        bottom_part,
        [((2, 2, 8, 4 * C), BF)],
        [VMEM] * 16,
        [pltpu.VMEM((7, 1, 32, 2 * C), BF), pltpu.VMEM((5, 2, 32, C), F32)],
    )(
        far, near, own, below, wa, ba, wb, bb, wd, bd, flags, hidden_far, hidden_near, top_taps, taps_far, taps_near
    )
    return out[None]


def solution(mesh):
    placed = (P("span", None, "row", None, None), P(), P(), P(), P(), P(), P(), P(), P())
    return jax.shard_map(
        per_device,
        mesh=mesh,
        in_specs=placed,
        out_specs=P("span", None, "row", None, None),
        check_vma=False,
    )
```

```python
import jax
import jax.numpy as jnp
from jax import lax
from jax.experimental import pallas as pl
from jax.experimental.pallas import tpu as pltpu
from jax.sharding import PartitionSpec as P

BF = jnp.bfloat16
F32 = jnp.float32
C = 128
VMEM = pl.BlockSpec(memory_space=pltpu.VMEM)
HBM = pl.BlockSpec(memory_space=pltpu.HBM)


def shifted(x, axis, by):
    peers = lax.axis_size(axis)
    pairs = [(i, i + by) for i in range(peers) if 0 <= i + by < peers]
    return lax.ppermute(x, axis, pairs)


def continues(lengths, order, slot):
    begin = jnp.int32(0)
    first = jnp.int32(0)
    for k in range(16):
        first = jnp.where(begin == slot, jnp.int32(1), first)
        begin = begin + lengths[order[k]]
    return 1 - first


def last_frames(features, out, sem):
    copies = [
        pltpu.make_async_copy(features.at[2 + f, pl.ds(4 * part, 4)], out.at[f, pl.ds(4 * part, 4)], sem.at[2 * f + part])
        for f in range(2)
        for part in range(2)
    ]
    for copy in copies:
        copy.start()
    for copy in copies:
        copy.wait()


def prepare(lengths, order, features, a, b, pa, pb, pairs, flags, smem, own, taps, sem):
    copies = [
        pltpu.make_async_copy(lengths, smem.at[0], sem.at[0]),
        pltpu.make_async_copy(order, smem.at[1], sem.at[1]),
        pltpu.make_async_copy(features.at[pl.ds(0, 3)], own, sem.at[2]),
    ]
    for i, src in enumerate((a, b)):
        for t in range(3):
            part = pl.ds(9 * t, 9)
            copies.append(pltpu.make_async_copy(src.at[part], taps.at[i, part], sem.at[3 + 3 * i + t]))
    for copy in copies:
        copy.start()
    for copy in copies[:3]:
        copy.wait()
    slot = lax.axis_index("span")
    block = lax.axis_index("row")
    values = (
        continues(smem.at[0], smem.at[1], slot),
        continues(smem.at[0], smem.at[1], slot - 1),
        (block > 0).astype(jnp.int32),
        (block < lax.axis_size("row") - 1).astype(jnp.int32),
    )
    for i, value in enumerate(values):
        flags[i] = jnp.full((8, C), value.astype(F32), F32)
    for f in range(3):
        for row in range(8):
            pairs[f, row // 2, :, pl.ds(row % 2 * C, C)] = own[f, row]
    for n, dst in enumerate((pa, pb)):
        for t in range(3):
            copies[3 + 3 * n + t].wait()
            for i in range(4):
                for w in range(3):
                    for j in range(2):
                        k = i - j
                        value = taps[n, t * 9 + k * 3 + w] if 0 <= k <= 2 else jnp.zeros((C, C), BF)
                        at = (i // 2 * 3 + t) * 2 + i % 2
                        dst[pl.ds(at * C, C), pl.ds((j * 3 + w) * C, C)] = value


def pack_up(far, near, own, flags, after, up, pairs):
    both = (flags[0, 0:1, :] * flags[1, 0:1, :]).astype(BF)
    for f in range(2):
        for row in range(8):
            value = far[f, row] * both
            pairs[f, row // 2, :, pl.ds(row % 2 * C, C)] = value
            if row >= 5:
                up[f, row - 5] = value
    for f in range(7):
        for row in range(5, 8):
            lanes = pl.ds(row % 2 * C, C)
            up[2 + f, row - 5] = near[f, row // 2, :, lanes] if f < 4 else own[f - 4, row // 2, :, lanes]


def pack_down(far, near, own, down):
    for f in range(9):
        for row in range(2):
            src, at = (far, f) if f < 2 else (near, f - 2) if f < 6 else (own, f - 6)
            down[f, row] = src[at, 0, :, pl.ds(row * C, C)]


def twice(bias):
    return jnp.concatenate([bias[...], bias[...]], axis=1)


def conv(blocks, fetch, weight, sides=(0, 1), lower=False):
    rows = len(blocks) * 32
    lhs = jnp.concatenate(
        [
            jnp.concatenate([fetch(f - 2 + t, q + side) for f, q in blocks], axis=0)
            for side in sides
            for t in range(3)
        ],
        axis=1,
    )
    rhs = weight[pl.ds(sides[0] * 6 * C, len(sides) * 6 * C), pl.ds(3 * C if lower else 0, 3 * C if lower else 6 * C)]
    y = jnp.dot(lhs, rhs, preferred_element_type=F32).reshape(len(blocks), 32, -1)
    col = lax.broadcasted_iota(jnp.int32, (1, 32, C), 1)
    out = []
    for at in range(0, y.shape[2], 3 * C):
        left = jnp.where(col == 0, 0.0, pltpu.roll(y[:, :, at : at + C], 1, 1))
        right = jnp.where(col == 31, 0.0, pltpu.roll(y[:, :, at + 2 * C : at + 3 * C], 31, 1))
        out.append(y[:, :, at + C : at + 2 * C] + left + right)
    return (out[0] if lower else jnp.concatenate(out, axis=2)).reshape(rows, -1)


def hidden_blocks(blocks, sums, bias, flags, put):
    lower = sums.shape[1] == C
    v = sums + (bias[...] if lower else twice(bias))
    v = v / (1.0 + jnp.exp(-v))
    keep, top, bottom = (flags[i, 0:1, :] for i in (0, 2, 3))
    one = jnp.ones_like(top)
    for i, (f, q) in enumerate(blocks):
        value = v[i * 32 : i * 32 + 32]
        if q == 0:
            value = value * top
        elif q == 1:
            value = value * jnp.concatenate([top, one], axis=1)
        elif q == 5:
            value = value * jnp.concatenate([one, bottom], axis=1)
        if f < 0:
            value = value * (keep if lower else jnp.concatenate([keep, keep], axis=1))
        put(f, q, value.astype(BF))


def mixed_blocks(blocks, sums, residual, bias, flags, put):
    lower = sums.shape[1] == C
    v = sums + (bias[...] if lower else twice(bias))
    keep, top = flags[0, 0:1, :], flags[2, 0:1, :]
    for i, (f, p) in enumerate(blocks):
        x = residual(f, p + 1).astype(F32)
        value = (x[:, C:] if lower else x) + v[i * 32 : i * 32 + 32]
        value = value.astype(BF).astype(F32)
        if f < 0:
            value = value * (keep if lower else jnp.concatenate([keep, keep], axis=1))
        if p == 0:
            put(f, 0, value * top)
        else:
            put(f, 2 * p - 1, value[:, :C])
            put(f, 2 * p, value[:, C:])


def column_taps(row):
    m = [row[pl.ds(k, 8, stride=4), :] for k in range(4)]
    first = lax.broadcasted_iota(jnp.int32, (8, C), 0) == 0
    before = jnp.where(first, 0.0, pltpu.roll(m[3], 1, 0))
    columns = ((before, m[1]), (m[0], m[2]), (m[1], m[3]))
    return jnp.concatenate([jnp.concatenate(pair, axis=0).astype(BF) for pair in columns], axis=1)


def own_feature(far, near, own):
    def feature(f, g):
        src, at = (far, f + 6) if f < -4 else (near, f + 4) if f < 0 else (own, f)
        return src[at, g - 2]

    return feature


def inner_near(arrived, own, wa, ba, wb, bb, flags, near, hidden, taps, m):
    keep = flags[0, 0:1, :].astype(BF)
    for f in range(4):
        for row in range(8):
            near[f, row // 2, :, pl.ds(row % 2 * C, C)] = arrived[f, row] * keep
    feature = own_feature(None, near, own)

    def put_hidden(f, q, value):
        hidden[f + 2, q - 2] = value

    def put_mixed(f, r, value):
        m[f, r - 3] = value

    for frames in ((-2, -1), (0, 1, 2)):
        blocks = [(f, q) for f in frames for q in (2, 3, 4)]
        hidden_blocks(blocks, conv(blocks, feature, wa), ba, flags, put_hidden)
    blocks = [(f, p) for f in range(3) for p in (2, 3)]
    sums = conv(blocks, lambda f, q: hidden[f + 2, q - 2], wb)
    mixed_blocks(blocks, sums, feature, bb, flags, put_mixed)
    for f in range(3):
        for r in range(4):
            taps[f, r] = column_taps(m.at[f, r])


def inner_far(far, near, wa, ba, flags, hidden):
    def put_hidden(f, q, value):
        hidden[f + 4, q - 2] = value

    blocks = [(f, q) for f in (-4, -3) for q in (2, 3, 4)]
    hidden_blocks(blocks, conv(blocks, own_feature(far, near, None), wa), ba, flags, put_hidden)


def inner_mixed(near, wb, bb, flags, hidden_far, hidden_near, taps, m):
    def hidden(f, q):
        return hidden_far[f + 4, q - 2] if f < -2 else hidden_near[f + 2, q - 2]

    def put_mixed(f, r, value):
        m[f + 2, r - 3] = value

    blocks = [(f, p) for f in (-2, -1) for p in (2, 3)]
    mixed_blocks(blocks, conv(blocks, hidden, wb), own_feature(None, near, None), bb, flags, put_mixed)
    for f in range(2):
        for r in range(4):
            taps[f, r] = column_taps(m.at[f, r])


HIDDEN = range(-4, 3)
MIXED = range(-2, 3)


def inner_hidden(hidden_far, hidden_near):
    def hidden(f, q):
        return hidden_far[f + 4, q - 2] if f < -2 else hidden_near[f + 2, q - 2]

    return hidden


def early_part(far, near, own, wa, wb, hidden_far, hidden_near, after, top_hidden, top_mixed, bottom_hidden, bottom_mixed):
    feature = own_feature(far, near, own)
    hidden = inner_hidden(hidden_far, hidden_near)
    top_hidden[...] = conv([(f, 1) for f in HIDDEN], feature, wa, (1,))
    top_mixed[...] = conv([(f, 1) for f in MIXED], hidden, wb, (1,))
    bottom_hidden[...] = conv([(f, 5) for f in HIDDEN], feature, wa, (0,))
    bottom_mixed[...] = conv([(f, 4) for f in MIXED], hidden, wb, (0,))


def top_part(far, near, own, above, wa, ba, wb, bb, flags, part_hidden, part_mixed, taps, h, m):
    inside = own_feature(far, near, own)

    def feature(f, g):
        if g >= 2:
            return inside(f, g)
        upper = jnp.zeros((32, C), BF) if g == 0 else above[f + 6, 1]
        return jnp.concatenate([upper, above[f + 6, 2 * g]], axis=1)

    def put_hidden(f, q, value):
        if q == 0:
            h[f + 4, 0, :, pl.ds(0, C)] = jnp.zeros((32, C), BF)
            h[f + 4, 0, :, pl.ds(C, C)] = value
        else:
            h[f + 4, 1] = value

    def put_mixed(f, r, value):
        m[f + 2, r] = value

    def hidden(f, q):
        return h[f + 4, q]

    blocks = [(f, 1) for f in HIDDEN]
    hidden_blocks(blocks, conv(blocks, feature, wa, (0,)) + part_hidden[...], ba, flags, put_hidden)
    blocks = [(f, 0) for f in HIDDEN]
    hidden_blocks(blocks, conv(blocks, feature, wa, lower=True), ba, flags, put_hidden)
    blocks = [(f, 1) for f in MIXED]
    mixed_blocks(blocks, conv(blocks, hidden, wb, (0,)) + part_mixed[...], feature, bb, flags, put_mixed)
    blocks = [(f, 0) for f in MIXED]
    mixed_blocks(blocks, conv(blocks, hidden, wb, lower=True), feature, bb, flags, put_mixed)
    for f in range(5):
        for r in range(3):
            taps[f, r] = column_taps(m.at[f, r])


def bottom_part(
    far, near, own, below, wa, ba, wb, bb, wd, bd, flags, part_hidden, part_mixed, top_taps, taps_far, taps_near, out, h, m
):
    def feature(f, g):
        return jnp.concatenate([below[f + 6, 0], below[f + 6, 1]], axis=1)

    def put_hidden(f, q, value):
        h[f + 4] = value

    def put_mixed(f, r, value):
        m[f + 2, r - 7] = value

    blocks = [(f, 5) for f in HIDDEN]
    hidden_blocks(blocks, conv(blocks, feature, wa, (1,)) + part_hidden[...], ba, flags, put_hidden)
    blocks = [(f, 4) for f in MIXED]
    sums = conv(blocks, lambda f, q: h[f + 4], wb, (1,)) + part_mixed[...]
    mixed_blocks(blocks, sums, own_feature(far, near, own), bb, flags, put_mixed)
    frames = []
    for f in range(5):
        rows = [top_taps[f, r] for r in range(3)] + [taps_far[f, r] if f < 2 else taps_near[f - 2, r] for r in range(4)]
        rows += [column_taps(m.at[f, r]) for r in range(2)]
        frames.append(
            jnp.concatenate(
                [jnp.concatenate([rows[2 * j + k] for k in range(3)], axis=1) for j in range(4)], axis=0
            )
        )
    lhs = jnp.concatenate([jnp.concatenate(frames[t : t + 3], axis=1) for t in (0, 2)], axis=0)
    v = jnp.dot(lhs, wd[...], preferred_element_type=F32) + bd[...]
    v = v.astype(BF).astype(F32)
    for t in range(2):
        for i in range(2):
            at = t * 64 + i * 32
            out[t, i] = jnp.concatenate([v[at + k * 8 : at + k * 8 + 8] for k in range(4)], axis=1).astype(BF)


def kernel(body, outs, ins, scratch=(), flops=0):
    return pl.pallas_call(
        body,
        name=body.__name__,
        out_shape=[jax.ShapeDtypeStruct(*o) for o in outs],
        in_specs=ins,
        out_specs=[VMEM] * len(outs),
        scratch_shapes=list(scratch),
        compiler_params=pltpu.CompilerParams(vmem_limit_bytes=24 << 20),
        cost_estimate=pl.CostEstimate(flops=flops, bytes_accessed=1 << 10, transcendentals=0),
    )


def per_device(
    features, clip_lengths, clip_order, weight_a, bias_a, weight_b, bias_b, weight_down, bias_down
):
    wd = weight_down.reshape(27 * C, C)
    ba, bb, bd = (b.reshape(1, C) for b in (bias_a, bias_b, bias_down))
    near = shifted(features[0], "span", 1)
    taps_a, taps_b = (w.reshape(27, C, C) for w in (weight_a, weight_b))
    stay = [
        pltpu.with_memory_space_constraint(x, pltpu.HBM)
        for x in (clip_lengths, clip_order, features[0], taps_a, taps_b)
    ]
    (tail,) = kernel(
        last_frames,
        [((2, 8, 32, C), BF)],
        [HBM],
        [pltpu.SemaphoreType.DMA((4,))],
    )(stay[2])
    far = shifted(tail, "span", 2)
    packed = ((12 * C, 6 * C), BF)
    wa, wb, own, flags = kernel(
        prepare,
        [packed, packed, ((3, 4, 32, 2 * C), BF), ((4, 8, C), F32)],
        [HBM] * 5,
        [
            pltpu.SMEM((2, 16), jnp.int32),
            pltpu.VMEM((3, 8, 32, C), BF),
            pltpu.VMEM((2, 27, C, C), BF),
            pltpu.SemaphoreType.DMA((9,)),
        ],
    )(*stay)
    near, hidden_near, taps_near = kernel(
        inner_near,
        [((4, 4, 32, 2 * C), BF), ((5, 3, 32, 2 * C), BF), ((3, 4, 16, 3 * C), BF)],
        [VMEM] * 7,
        [pltpu.VMEM((3, 4, 32, C), F32)],
    )(near, own, wa, ba, wb, bb, flags)
    up, far = kernel(
        pack_up, [((9, 3, 32, C), BF), ((2, 4, 32, 2 * C), BF)], [VMEM] * 5
    )(far, near, own, flags, taps_near)
    above = shifted(up, "row", 1)
    (down,) = kernel(pack_down, [((9, 2, 32, C), BF)], [VMEM] * 3)(far, near, own)
    below = shifted(down, "row", -1)
    (hidden_far,) = kernel(inner_far, [((2, 3, 32, 2 * C), BF)], [VMEM] * 5)(far, near, wa, ba, flags)
    (taps_far,) = kernel(
        inner_mixed, [((2, 4, 16, 3 * C), BF)], [VMEM] * 6, [pltpu.VMEM((2, 4, 32, C), F32)]
    )(near, wb, bb, flags, hidden_far, hidden_near)
    sums_hidden = ((7 * 32, 2 * C), F32)
    sums_mixed = ((5 * 32, 2 * C), F32)
    top_hidden, top_mixed, bottom_hidden, bottom_mixed = kernel(
        early_part, [sums_hidden, sums_mixed] * 2, [VMEM] * 8
    )(far, near, own, wa, wb, hidden_far, hidden_near, taps_far)
    (top_taps,) = kernel(
        top_part,
        [((5, 3, 16, 3 * C), BF)],
        [VMEM] * 11,
        [pltpu.VMEM((7, 2, 32, 2 * C), BF), pltpu.VMEM((5, 3, 32, C), F32)],
    )(far, near, own, above, wa, ba, wb, bb, flags, top_hidden, top_mixed)
    (out,) = kernel(
        bottom_part,
        [((2, 2, 8, 4 * C), BF)],
        [VMEM] * 16,
        [pltpu.VMEM((7, 32, 2 * C), BF), pltpu.VMEM((5, 2, 32, C), F32)],
    )(
        far, near, own, below, wa, ba, wb, bb, wd, bd, flags, bottom_hidden, bottom_mixed, top_taps, taps_far, taps_near
    )
    return out[None]


def solution(mesh):
    placed = (P("span", None, "row", None, None), P(), P(), P(), P(), P(), P(), P(), P())
    return jax.shard_map(
        per_device,
        mesh=mesh,
        in_specs=placed,
        out_specs=P("span", None, "row", None, None),
        check_vma=False,
    )
```

```python
import jax
import jax.numpy as jnp
from jax import lax
from jax.experimental import pallas as pl
from jax.experimental.pallas import tpu as pltpu
from jax.sharding import PartitionSpec as P

BF = jnp.bfloat16
F32 = jnp.float32
C = 128
VMEM = pl.BlockSpec(memory_space=pltpu.VMEM)
HBM = pl.BlockSpec(memory_space=pltpu.HBM)


def shifted(x, axis, by):
    peers = lax.axis_size(axis)
    pairs = [(i, i + by) for i in range(peers) if 0 <= i + by < peers]
    return lax.ppermute(x, axis, pairs)


def continues(lengths, order, slot):
    begin = jnp.int32(0)
    first = jnp.int32(0)
    for k in range(16):
        first = jnp.where(begin == slot, jnp.int32(1), first)
        begin = begin + lengths[order[k]]
    return 1 - first


def last_frames(features, out, sem):
    copies = [
        pltpu.make_async_copy(features.at[2 + f, pl.ds(4 * part, 4)], out.at[f, pl.ds(4 * part, 4)], sem.at[2 * f + part])
        for f in range(2)
        for part in range(2)
    ]
    for copy in copies:
        copy.start()
    for copy in copies:
        copy.wait()


def prepare(lengths, order, features, a, b, pa, pb, pairs, flags, smem, own, taps, sem):
    copies = [
        pltpu.make_async_copy(lengths, smem.at[0], sem.at[0]),
        pltpu.make_async_copy(order, smem.at[1], sem.at[1]),
        pltpu.make_async_copy(features.at[pl.ds(0, 3)], own, sem.at[2]),
    ]
    for i, src in enumerate((a, b)):
        for t in range(3):
            part = pl.ds(9 * t, 9)
            copies.append(pltpu.make_async_copy(src.at[part], taps.at[i, part], sem.at[3 + 3 * i + t]))
    for copy in copies:
        copy.start()
    for copy in copies[:3]:
        copy.wait()
    slot = lax.axis_index("span")
    block = lax.axis_index("row")
    values = (
        continues(smem.at[0], smem.at[1], slot),
        continues(smem.at[0], smem.at[1], slot - 1),
        (block > 0).astype(jnp.int32),
        (block < lax.axis_size("row") - 1).astype(jnp.int32),
    )
    for i, value in enumerate(values):
        flags[i] = jnp.full((8, C), value.astype(F32), F32)
    for f in range(3):
        for row in range(8):
            pairs[f, row // 2, :, pl.ds(row % 2 * C, C)] = own[f, row]
    for n, dst in enumerate((pa, pb)):
        for t in range(3):
            copies[3 + 3 * n + t].wait()
            for i in range(4):
                for w in range(3):
                    for j in range(2):
                        k = i - j
                        value = taps[n, t * 9 + k * 3 + w] if 0 <= k <= 2 else jnp.zeros((C, C), BF)
                        at = (i // 2 * 3 + t) * 2 + i % 2
                        dst[pl.ds(at * C, C), pl.ds((j * 3 + w) * C, C)] = value


def pack_up(far, near, own, flags, after, up, pairs):
    both = (flags[0, 0:1, :] * flags[1, 0:1, :]).astype(BF)
    for f in range(2):
        for row in range(8):
            value = far[f, row] * both
            pairs[f, row // 2, :, pl.ds(row % 2 * C, C)] = value
            if row >= 5:
                up[f, row - 5] = value
    for f in range(7):
        for row in range(5, 8):
            lanes = pl.ds(row % 2 * C, C)
            up[2 + f, row - 5] = near[f, row // 2, :, lanes] if f < 4 else own[f - 4, row // 2, :, lanes]


def pack_down(far, near, own, down):
    for f in range(9):
        for row in range(2):
            src, at = (far, f) if f < 2 else (near, f - 2) if f < 6 else (own, f - 6)
            down[f, row] = src[at, 0, :, pl.ds(row * C, C)]


def twice(bias):
    return jnp.concatenate([bias[...], bias[...]], axis=1)


def conv(blocks, fetch, weight, sides=(0, 1), lower=False):
    rows = len(blocks) * 32
    lhs = jnp.concatenate(
        [
            jnp.concatenate([fetch(f - 2 + t, q + side) for f, q in blocks], axis=0)
            for side in sides
            for t in range(3)
        ],
        axis=1,
    )
    rhs = weight[pl.ds(sides[0] * 6 * C, len(sides) * 6 * C), pl.ds(3 * C if lower else 0, 3 * C if lower else 6 * C)]
    y = jnp.dot(lhs, rhs, preferred_element_type=F32).reshape(len(blocks), 32, -1)
    col = lax.broadcasted_iota(jnp.int32, (1, 32, C), 1)
    out = []
    for at in range(0, y.shape[2], 3 * C):
        left = jnp.where(col == 0, 0.0, pltpu.roll(y[:, :, at : at + C], 1, 1))
        right = jnp.where(col == 31, 0.0, pltpu.roll(y[:, :, at + 2 * C : at + 3 * C], 31, 1))
        out.append(y[:, :, at + C : at + 2 * C] + left + right)
    return (out[0] if lower else jnp.concatenate(out, axis=2)).reshape(rows, -1)


def hidden_blocks(blocks, sums, bias, flags, put):
    lower = sums.shape[1] == C
    v = sums + (bias[...] if lower else twice(bias))
    v = v / (1.0 + jnp.exp(-v))
    keep, top, bottom = (flags[i, 0:1, :] for i in (0, 2, 3))
    one = jnp.ones_like(top)
    for i, (f, q) in enumerate(blocks):
        value = v[i * 32 : i * 32 + 32]
        if q == 0:
            value = value * top
        elif q == 1:
            value = value * jnp.concatenate([top, one], axis=1)
        elif q == 5:
            value = value * jnp.concatenate([one, bottom], axis=1)
        if f < 0:
            value = value * (keep if lower else jnp.concatenate([keep, keep], axis=1))
        put(f, q, value.astype(BF))


def mixed_blocks(blocks, sums, residual, bias, flags, put):
    lower = sums.shape[1] == C
    v = sums + (bias[...] if lower else twice(bias))
    keep, top = flags[0, 0:1, :], flags[2, 0:1, :]
    for i, (f, p) in enumerate(blocks):
        x = residual(f, p + 1).astype(F32)
        value = (x[:, C:] if lower else x) + v[i * 32 : i * 32 + 32]
        value = value.astype(BF).astype(F32)
        if f < 0:
            value = value * (keep if lower else jnp.concatenate([keep, keep], axis=1))
        if p == 0:
            put(f, 0, value * top)
        else:
            put(f, 2 * p - 1, value[:, :C])
            put(f, 2 * p, value[:, C:])


def column_taps(row):
    m = [row[pl.ds(k, 8, stride=4), :] for k in range(4)]
    first = lax.broadcasted_iota(jnp.int32, (8, C), 0) == 0
    before = jnp.where(first, 0.0, pltpu.roll(m[3], 1, 0))
    columns = ((before, m[1]), (m[0], m[2]), (m[1], m[3]))
    return jnp.concatenate([jnp.concatenate(pair, axis=0).astype(BF) for pair in columns], axis=1)


def own_feature(far, near, own):
    def feature(f, g):
        src, at = (far, f + 6) if f < -4 else (near, f + 4) if f < 0 else (own, f)
        return src[at, g - 2]

    return feature


def inner_near(arrived, own, wa, ba, wb, bb, flags, near, hidden, taps, m):
    keep = flags[0, 0:1, :].astype(BF)
    for f in range(4):
        for row in range(8):
            near[f, row // 2, :, pl.ds(row % 2 * C, C)] = arrived[f, row] * keep
    feature = own_feature(None, near, own)

    def put_hidden(f, q, value):
        hidden[f + 2, q - 2] = value

    def put_mixed(f, r, value):
        m[f, r - 3] = value

    for frames in ((-2, -1), (0, 1, 2)):
        blocks = [(f, q) for f in frames for q in (2, 3, 4)]
        hidden_blocks(blocks, conv(blocks, feature, wa), ba, flags, put_hidden)
    blocks = [(f, p) for f in range(3) for p in (2, 3)]
    sums = conv(blocks, lambda f, q: hidden[f + 2, q - 2], wb)
    mixed_blocks(blocks, sums, feature, bb, flags, put_mixed)
    for f in range(3):
        for r in range(4):
            taps[f, r] = column_taps(m.at[f, r])


def inner_far(far, near, wa, ba, flags, hidden):
    def put_hidden(f, q, value):
        hidden[f + 4, q - 2] = value

    blocks = [(f, q) for f in (-4, -3) for q in (2, 3, 4)]
    hidden_blocks(blocks, conv(blocks, own_feature(far, near, None), wa), ba, flags, put_hidden)


def inner_mixed(near, wb, bb, flags, hidden_far, hidden_near, taps, m):
    def hidden(f, q):
        return hidden_far[f + 4, q - 2] if f < -2 else hidden_near[f + 2, q - 2]

    def put_mixed(f, r, value):
        m[f + 2, r - 3] = value

    blocks = [(f, p) for f in (-2, -1) for p in (2, 3)]
    mixed_blocks(blocks, conv(blocks, hidden, wb), own_feature(None, near, None), bb, flags, put_mixed)
    for f in range(2):
        for r in range(4):
            taps[f, r] = column_taps(m.at[f, r])


HIDDEN = range(-4, 3)
MIXED = range(-2, 3)


def inner_hidden(hidden_far, hidden_near):
    def hidden(f, q):
        return hidden_far[f + 4, q - 2] if f < -2 else hidden_near[f + 2, q - 2]

    return hidden


def early_part(far, near, own, wa, wb, hidden_far, hidden_near, after, top_hidden, top_mixed, bottom_hidden, bottom_mixed):
    feature = own_feature(far, near, own)
    hidden = inner_hidden(hidden_far, hidden_near)
    top_hidden[...] = conv([(f, 1) for f in HIDDEN], feature, wa, (1,))
    top_mixed[...] = conv([(f, 1) for f in MIXED], hidden, wb, (1,))
    bottom_hidden[...] = conv([(f, 5) for f in HIDDEN], feature, wa, (0,))
    bottom_mixed[...] = conv([(f, 4) for f in MIXED], hidden, wb, (0,))


def top_part(
    far, near, own, above, wa, ba, wb, bb, wd, bd, flags, part_hidden, part_mixed, taps_far, taps_near, sums, h, m
):
    inside = own_feature(far, near, own)

    def feature(f, g):
        if g >= 2:
            return inside(f, g)
        upper = jnp.zeros((32, C), BF) if g == 0 else above[f + 6, 1]
        return jnp.concatenate([upper, above[f + 6, 2 * g]], axis=1)

    def put_hidden(f, q, value):
        if q == 0:
            h[f + 4, 0, :, pl.ds(0, C)] = jnp.zeros((32, C), BF)
            h[f + 4, 0, :, pl.ds(C, C)] = value
        else:
            h[f + 4, 1] = value

    def put_mixed(f, r, value):
        m[f + 2, r] = value

    def hidden(f, q):
        return h[f + 4, q]

    blocks = [(f, 1) for f in HIDDEN]
    hidden_blocks(blocks, conv(blocks, feature, wa, (0,)) + part_hidden[...], ba, flags, put_hidden)
    blocks = [(f, 0) for f in HIDDEN]
    hidden_blocks(blocks, conv(blocks, feature, wa, lower=True), ba, flags, put_hidden)
    blocks = [(f, 1) for f in MIXED]
    mixed_blocks(blocks, conv(blocks, hidden, wb, (0,)) + part_mixed[...], feature, bb, flags, put_mixed)
    blocks = [(f, 0) for f in MIXED]
    mixed_blocks(blocks, conv(blocks, hidden, wb, lower=True), feature, bb, flags, put_mixed)
    none = jnp.zeros((16, 3 * C), BF)
    frames = []
    for f in range(5):
        rows = [column_taps(m.at[f, r]) for r in range(3)]
        rows += [taps_far[f, r] if f < 2 else taps_near[f - 2, r] for r in range(4)] + [none, none]
        frames.append(
            jnp.concatenate(
                [jnp.concatenate([rows[2 * j + k] for k in range(3)], axis=1) for j in range(4)], axis=0
            )
        )
    lhs = jnp.concatenate([jnp.concatenate(frames[t : t + 3], axis=1) for t in (0, 2)], axis=0)
    sums[...] = jnp.dot(lhs, wd[...], preferred_element_type=F32) + bd[...]


def bottom_part(
    far, near, own, below, wa, ba, wb, bb, wd, flags, part_hidden, part_mixed, sums, out, h, m
):
    def feature(f, g):
        return jnp.concatenate([below[f + 6, 0], below[f + 6, 1]], axis=1)

    def put_hidden(f, q, value):
        h[f + 4] = value

    def put_mixed(f, r, value):
        m[f + 2, r - 7] = value

    blocks = [(f, 5) for f in HIDDEN]
    hidden_blocks(blocks, conv(blocks, feature, wa, (1,)) + part_hidden[...], ba, flags, put_hidden)
    blocks = [(f, 4) for f in MIXED]
    total = conv(blocks, lambda f, q: h[f + 4], wb, (1,)) + part_mixed[...]
    mixed_blocks(blocks, total, own_feature(far, near, own), bb, flags, put_mixed)
    rows = [jnp.concatenate([column_taps(m.at[f, r]) for r in range(2)], axis=1) for f in range(5)]
    low = sum(
        jnp.dot(
            jnp.concatenate([rows[t], rows[t + 2]], axis=0),
            wd[pl.ds((9 * t + 3) * C, 6 * C), :],
            preferred_element_type=F32,
        )
        for t in range(3)
    )
    for t in range(2):
        for i in range(2):
            at = t * 64 + i * 32
            v = sums[at : at + 32]
            if i == 1:
                v = jnp.concatenate([v[:16], v[16:] + low[t * 16 : t * 16 + 16]], axis=0)
            out[t, i] = jnp.concatenate([v[k * 8 : k * 8 + 8] for k in range(4)], axis=1).astype(BF)


def kernel(body, outs, ins, scratch=(), flops=0):
    return pl.pallas_call(
        body,
        name=body.__name__,
        out_shape=[jax.ShapeDtypeStruct(*o) for o in outs],
        in_specs=ins,
        out_specs=[VMEM] * len(outs),
        scratch_shapes=list(scratch),
        compiler_params=pltpu.CompilerParams(vmem_limit_bytes=24 << 20),
        cost_estimate=pl.CostEstimate(flops=flops, bytes_accessed=1 << 10, transcendentals=0),
    )


def per_device(
    features, clip_lengths, clip_order, weight_a, bias_a, weight_b, bias_b, weight_down, bias_down
):
    wd = weight_down.reshape(27 * C, C)
    ba, bb, bd = (b.reshape(1, C) for b in (bias_a, bias_b, bias_down))
    near = shifted(features[0], "span", 1)
    taps_a, taps_b = (w.reshape(27, C, C) for w in (weight_a, weight_b))
    stay = [
        pltpu.with_memory_space_constraint(x, pltpu.HBM)
        for x in (clip_lengths, clip_order, features[0], taps_a, taps_b)
    ]
    (tail,) = kernel(
        last_frames,
        [((2, 8, 32, C), BF)],
        [HBM],
        [pltpu.SemaphoreType.DMA((4,))],
    )(stay[2])
    far = shifted(tail, "span", 2)
    packed = ((12 * C, 6 * C), BF)
    wa, wb, own, flags = kernel(
        prepare,
        [packed, packed, ((3, 4, 32, 2 * C), BF), ((4, 8, C), F32)],
        [HBM] * 5,
        [
            pltpu.SMEM((2, 16), jnp.int32),
            pltpu.VMEM((3, 8, 32, C), BF),
            pltpu.VMEM((2, 27, C, C), BF),
            pltpu.SemaphoreType.DMA((9,)),
        ],
    )(*stay)
    near, hidden_near, taps_near = kernel(
        inner_near,
        [((4, 4, 32, 2 * C), BF), ((5, 3, 32, 2 * C), BF), ((3, 4, 16, 3 * C), BF)],
        [VMEM] * 7,
        [pltpu.VMEM((3, 4, 32, C), F32)],
    )(near, own, wa, ba, wb, bb, flags)
    up, far = kernel(
        pack_up, [((9, 3, 32, C), BF), ((2, 4, 32, 2 * C), BF)], [VMEM] * 5
    )(far, near, own, flags, taps_near)
    above = shifted(up, "row", 1)
    (down,) = kernel(pack_down, [((9, 2, 32, C), BF)], [VMEM] * 3)(far, near, own)
    below = shifted(down, "row", -1)
    (hidden_far,) = kernel(inner_far, [((2, 3, 32, 2 * C), BF)], [VMEM] * 5)(far, near, wa, ba, flags)
    (taps_far,) = kernel(
        inner_mixed, [((2, 4, 16, 3 * C), BF)], [VMEM] * 6, [pltpu.VMEM((2, 4, 32, C), F32)]
    )(near, wb, bb, flags, hidden_far, hidden_near)
    sums_hidden = ((7 * 32, 2 * C), F32)
    sums_mixed = ((5 * 32, 2 * C), F32)
    top_hidden, top_mixed, bottom_hidden, bottom_mixed = kernel(
        early_part, [sums_hidden, sums_mixed] * 2, [VMEM] * 8
    )(far, near, own, wa, wb, hidden_far, hidden_near, taps_far)
    (sums,) = kernel(
        top_part,
        [((128, C), F32)],
        [VMEM] * 15,
        [pltpu.VMEM((7, 2, 32, 2 * C), BF), pltpu.VMEM((5, 3, 32, C), F32)],
    )(far, near, own, above, wa, ba, wb, bb, wd, bd, flags, top_hidden, top_mixed, taps_far, taps_near)
    (out,) = kernel(
        bottom_part,
        [((2, 2, 8, 4 * C), BF)],
        [VMEM] * 13,
        [pltpu.VMEM((7, 32, 2 * C), BF), pltpu.VMEM((5, 2, 32, C), F32)],
    )(far, near, own, below, wa, ba, wb, bb, wd, flags, bottom_hidden, bottom_mixed, sums)
    return out[None]


def solution(mesh):
    placed = (P("span", None, "row", None, None), P(), P(), P(), P(), P(), P(), P(), P())
    return jax.shard_map(
        per_device,
        mesh=mesh,
        in_specs=placed,
        out_specs=P("span", None, "row", None, None),
        check_vma=False,
    )
```

```python
import jax
import jax.numpy as jnp
from jax import lax
from jax.experimental import pallas as pl
from jax.experimental.pallas import tpu as pltpu
from jax.sharding import PartitionSpec as P

BF = jnp.bfloat16
F32 = jnp.float32
C = 128
VMEM = pl.BlockSpec(memory_space=pltpu.VMEM)
HBM = pl.BlockSpec(memory_space=pltpu.HBM)


def shifted(x, axis, by):
    peers = lax.axis_size(axis)
    pairs = [(i, i + by) for i in range(peers) if 0 <= i + by < peers]
    return lax.ppermute(x, axis, pairs)


def continues(lengths, order, slot):
    begin = jnp.int32(0)
    first = jnp.int32(0)
    for k in range(16):
        first = jnp.where(begin == slot, jnp.int32(1), first)
        begin = begin + lengths[order[k]]
    return 1 - first


def last_frames(features, out, sem):
    copies = [
        pltpu.make_async_copy(features.at[2 + f, pl.ds(4 * part, 4)], out.at[f, pl.ds(4 * part, 4)], sem.at[2 * f + part])
        for f in range(2)
        for part in range(2)
    ]
    for copy in copies:
        copy.start()
    for copy in copies:
        copy.wait()


def prepare(lengths, order, features, a, b, pa, pb, pairs, flags, smem, own, taps, sem):
    copies = [
        pltpu.make_async_copy(lengths, smem.at[0], sem.at[0]),
        pltpu.make_async_copy(order, smem.at[1], sem.at[1]),
        pltpu.make_async_copy(features.at[pl.ds(0, 3)], own, sem.at[2]),
    ]
    for i, src in enumerate((a, b)):
        for t in range(3):
            part = pl.ds(9 * t, 9)
            copies.append(pltpu.make_async_copy(src.at[part], taps.at[i, part], sem.at[3 + 3 * i + t]))
    for copy in copies:
        copy.start()
    for copy in copies[:3]:
        copy.wait()
    slot = lax.axis_index("span")
    block = lax.axis_index("row")
    values = (
        continues(smem.at[0], smem.at[1], slot),
        continues(smem.at[0], smem.at[1], slot - 1),
        (block > 0).astype(jnp.int32),
        (block < lax.axis_size("row") - 1).astype(jnp.int32),
    )
    for i, value in enumerate(values):
        flags[i] = jnp.full((8, C), value.astype(F32), F32)
    for f in range(3):
        for row in range(8):
            pairs[f, row // 2, :, pl.ds(row % 2 * C, C)] = own[f, row]
    for n, dst in enumerate((pa, pb)):
        for t in range(3):
            copies[3 + 3 * n + t].wait()
            for i in range(4):
                for w in range(3):
                    for j in range(2):
                        k = i - j
                        value = taps[n, t * 9 + k * 3 + w] if 0 <= k <= 2 else jnp.zeros((C, C), BF)
                        at = (i // 2 * 3 + t) * 2 + i % 2
                        dst[pl.ds(at * C, C), pl.ds((j * 3 + w) * C, C)] = value


def pack_up(far, near, own, flags, after, up, pairs):
    both = (flags[0, 0:1, :] * flags[1, 0:1, :]).astype(BF)
    for f in range(2):
        for row in range(8):
            value = far[f, row] * both
            pairs[f, row // 2, :, pl.ds(row % 2 * C, C)] = value
            if row >= 5:
                up[f, row - 5] = value
    for f in range(7):
        for row in range(5, 8):
            lanes = pl.ds(row % 2 * C, C)
            up[2 + f, row - 5] = near[f, row // 2, :, lanes] if f < 4 else own[f - 4, row // 2, :, lanes]


def pack_down(far, near, own, down):
    for f in range(9):
        for row in range(2):
            src, at = (far, f) if f < 2 else (near, f - 2) if f < 6 else (own, f - 6)
            down[f, row] = src[at, 0, :, pl.ds(row * C, C)]


def twice(bias):
    return jnp.concatenate([bias[...], bias[...]], axis=1)


def conv(blocks, fetch, weight, sides=(0, 1), lower=False):
    rows = len(blocks) * 32
    lhs = jnp.concatenate(
        [
            jnp.concatenate([fetch(f - 2 + t, q + side) for f, q in blocks], axis=0)
            for side in sides
            for t in range(3)
        ],
        axis=1,
    )
    rhs = weight[pl.ds(sides[0] * 6 * C, len(sides) * 6 * C), pl.ds(3 * C if lower else 0, 3 * C if lower else 6 * C)]
    y = jnp.dot(lhs, rhs, preferred_element_type=F32).reshape(len(blocks), 32, -1)
    col = lax.broadcasted_iota(jnp.int32, (1, 32, C), 1)
    out = []
    for at in range(0, y.shape[2], 3 * C):
        left = jnp.where(col == 0, 0.0, pltpu.roll(y[:, :, at : at + C], 1, 1))
        right = jnp.where(col == 31, 0.0, pltpu.roll(y[:, :, at + 2 * C : at + 3 * C], 31, 1))
        out.append(y[:, :, at + C : at + 2 * C] + left + right)
    return (out[0] if lower else jnp.concatenate(out, axis=2)).reshape(rows, -1)


def hidden_blocks(blocks, sums, bias, flags, put):
    lower = sums.shape[1] == C
    v = sums + (bias[...] if lower else twice(bias))
    v = v / (1.0 + jnp.exp(-v))
    keep, top, bottom = (flags[i, 0:1, :] for i in (0, 2, 3))
    one = jnp.ones_like(top)
    for i, (f, q) in enumerate(blocks):
        value = v[i * 32 : i * 32 + 32]
        if q == 0:
            value = value * top
        elif q == 1:
            value = value * jnp.concatenate([top, one], axis=1)
        elif q == 5:
            value = value * jnp.concatenate([one, bottom], axis=1)
        if f < 0:
            value = value * (keep if lower else jnp.concatenate([keep, keep], axis=1))
        put(f, q, value.astype(BF))


def mixed_blocks(blocks, sums, residual, bias, flags, put):
    lower = sums.shape[1] == C
    v = sums + (bias[...] if lower else twice(bias))
    keep, top = flags[0, 0:1, :], flags[2, 0:1, :]
    for i, (f, p) in enumerate(blocks):
        x = residual(f, p + 1).astype(F32)
        value = (x[:, C:] if lower else x) + v[i * 32 : i * 32 + 32]
        value = value.astype(BF).astype(F32)
        if f < 0:
            value = value * (keep if lower else jnp.concatenate([keep, keep], axis=1))
        if p == 0:
            put(f, 0, value * top)
        else:
            put(f, 2 * p - 1, value[:, :C])
            put(f, 2 * p, value[:, C:])


def column_taps(row):
    m = [row[pl.ds(k, 8, stride=4), :] for k in range(4)]
    first = lax.broadcasted_iota(jnp.int32, (8, C), 0) == 0
    before = jnp.where(first, 0.0, pltpu.roll(m[3], 1, 0))
    columns = ((before, m[1]), (m[0], m[2]), (m[1], m[3]))
    return jnp.concatenate([jnp.concatenate(pair, axis=0).astype(BF) for pair in columns], axis=1)


def own_feature(far, near, own):
    def feature(f, g):
        src, at = (far, f + 6) if f < -4 else (near, f + 4) if f < 0 else (own, f)
        return src[at, g - 2]

    return feature


def inner_near(arrived, own, wa, ba, wb, bb, flags, near, hidden, taps, m):
    keep = flags[0, 0:1, :].astype(BF)
    for f in range(4):
        for row in range(8):
            near[f, row // 2, :, pl.ds(row % 2 * C, C)] = arrived[f, row] * keep
    feature = own_feature(None, near, own)

    def put_hidden(f, q, value):
        hidden[f + 2, q - 2] = value

    def put_mixed(f, r, value):
        m[f, r - 3] = value

    for frames in ((-2, -1), (0, 1, 2)):
        blocks = [(f, q) for f in frames for q in (2, 3, 4)]
        hidden_blocks(blocks, conv(blocks, feature, wa), ba, flags, put_hidden)
    blocks = [(f, p) for f in range(3) for p in (2, 3)]
    sums = conv(blocks, lambda f, q: hidden[f + 2, q - 2], wb)
    mixed_blocks(blocks, sums, feature, bb, flags, put_mixed)
    for f in range(3):
        for r in range(4):
            taps[f, r] = column_taps(m.at[f, r])


def inner_far(far, near, wa, ba, flags, hidden):
    def put_hidden(f, q, value):
        hidden[f + 4, q - 2] = value

    blocks = [(f, q) for f in (-4, -3) for q in (2, 3, 4)]
    hidden_blocks(blocks, conv(blocks, own_feature(far, near, None), wa), ba, flags, put_hidden)


def inner_mixed(near, wb, bb, flags, hidden_far, hidden_near, taps, m):
    def hidden(f, q):
        return hidden_far[f + 4, q - 2] if f < -2 else hidden_near[f + 2, q - 2]

    def put_mixed(f, r, value):
        m[f + 2, r - 3] = value

    blocks = [(f, p) for f in (-2, -1) for p in (2, 3)]
    mixed_blocks(blocks, conv(blocks, hidden, wb), own_feature(None, near, None), bb, flags, put_mixed)
    for f in range(2):
        for r in range(4):
            taps[f, r] = column_taps(m.at[f, r])


HIDDEN = range(-4, 3)
MIXED = range(-2, 3)


def inner_hidden(hidden_far, hidden_near):
    def hidden(f, q):
        return hidden_far[f + 4, q - 2] if f < -2 else hidden_near[f + 2, q - 2]

    return hidden


def early_part(
    far, near, own, wa, wb, wd, hidden_far, hidden_near, after, top_hidden, top_mixed, bottom_hidden, bottom_mixed, low
):
    feature = own_feature(far, near, own)
    hidden = inner_hidden(hidden_far, hidden_near)
    top_hidden[...] = conv([(f, 1) for f in HIDDEN], feature, wa, (1,))
    top_mixed[...] = conv([(f, 1) for f in MIXED], hidden, wb, (1,))
    bottom_hidden[...] = conv([(f, 5) for f in HIDDEN], feature, wa, (0,))
    bottom_mixed[...] = conv([(f, 4) for f in MIXED], hidden, wb, (0,))
    for t in range(3):
        low[:, pl.ds(t * C, C)] = wd[pl.ds((9 * t + 3) * C, 6 * C), :]


def top_part(
    far, near, own, above, wa, ba, wb, bb, wd, bd, flags, part_hidden, part_mixed, taps_far, taps_near, sums, h, m
):
    inside = own_feature(far, near, own)

    def feature(f, g):
        if g >= 2:
            return inside(f, g)
        upper = jnp.zeros((32, C), BF) if g == 0 else above[f + 6, 1]
        return jnp.concatenate([upper, above[f + 6, 2 * g]], axis=1)

    def put_hidden(f, q, value):
        if q == 0:
            h[f + 4, 0, :, pl.ds(0, C)] = jnp.zeros((32, C), BF)
            h[f + 4, 0, :, pl.ds(C, C)] = value
        else:
            h[f + 4, 1] = value

    def put_mixed(f, r, value):
        m[f + 2, r] = value

    def hidden(f, q):
        return h[f + 4, q]

    blocks = [(f, 1) for f in HIDDEN]
    hidden_blocks(blocks, conv(blocks, feature, wa, (0,)) + part_hidden[...], ba, flags, put_hidden)
    blocks = [(f, 0) for f in HIDDEN]
    hidden_blocks(blocks, conv(blocks, feature, wa, lower=True), ba, flags, put_hidden)
    blocks = [(f, 1) for f in MIXED]
    mixed_blocks(blocks, conv(blocks, hidden, wb, (0,)) + part_mixed[...], feature, bb, flags, put_mixed)
    blocks = [(f, 0) for f in MIXED]
    mixed_blocks(blocks, conv(blocks, hidden, wb, lower=True), feature, bb, flags, put_mixed)
    none = jnp.zeros((16, 3 * C), BF)
    frames = []
    for f in range(5):
        rows = [column_taps(m.at[f, r]) for r in range(3)]
        rows += [taps_far[f, r] if f < 2 else taps_near[f - 2, r] for r in range(4)] + [none, none]
        frames.append(
            jnp.concatenate(
                [jnp.concatenate([rows[2 * j + k] for k in range(3)], axis=1) for j in range(4)], axis=0
            )
        )
    lhs = jnp.concatenate([jnp.concatenate(frames[t : t + 3], axis=1) for t in (0, 2)], axis=0)
    sums[...] = jnp.dot(lhs, wd[...], preferred_element_type=F32) + bd[...]


def bottom_part(
    far, near, own, below, wa, ba, wb, bb, wlow, flags, part_hidden, part_mixed, sums, out, h, m
):
    def feature(f, g):
        return jnp.concatenate([below[f + 6, 0], below[f + 6, 1]], axis=1)

    def put_hidden(f, q, value):
        h[f + 4] = value

    def put_mixed(f, r, value):
        m[f + 2, r - 7] = value

    blocks = [(f, 5) for f in HIDDEN]
    hidden_blocks(blocks, conv(blocks, feature, wa, (1,)) + part_hidden[...], ba, flags, put_hidden)
    blocks = [(f, 4) for f in MIXED]
    total = conv(blocks, lambda f, q: h[f + 4], wb, (1,)) + part_mixed[...]
    mixed_blocks(blocks, total, own_feature(far, near, own), bb, flags, put_mixed)
    rows = [jnp.concatenate([column_taps(m.at[f, r]) for r in range(2)], axis=1) for f in range(5)]
    y = jnp.dot(jnp.concatenate(rows, axis=0), wlow[...], preferred_element_type=F32)
    low = [sum(y[(2 * t + k) * 16 : (2 * t + k) * 16 + 16, k * C : k * C + C] for k in range(3)) for t in range(2)]
    for t in range(2):
        for i in range(2):
            at = t * 64 + i * 32
            v = sums[at : at + 32]
            if i == 1:
                v = jnp.concatenate([v[:16], v[16:] + low[t]], axis=0)
            out[t, i] = jnp.concatenate([v[k * 8 : k * 8 + 8] for k in range(4)], axis=1).astype(BF)


def kernel(body, outs, ins, scratch=(), flops=0):
    return pl.pallas_call(
        body,
        name=body.__name__,
        out_shape=[jax.ShapeDtypeStruct(*o) for o in outs],
        in_specs=ins,
        out_specs=[VMEM] * len(outs),
        scratch_shapes=list(scratch),
        compiler_params=pltpu.CompilerParams(vmem_limit_bytes=24 << 20),
        cost_estimate=pl.CostEstimate(flops=flops, bytes_accessed=1 << 10, transcendentals=0),
    )


def per_device(
    features, clip_lengths, clip_order, weight_a, bias_a, weight_b, bias_b, weight_down, bias_down
):
    wd = weight_down.reshape(27 * C, C)
    ba, bb, bd = (b.reshape(1, C) for b in (bias_a, bias_b, bias_down))
    near = shifted(features[0], "span", 1)
    taps_a, taps_b = (w.reshape(27, C, C) for w in (weight_a, weight_b))
    stay = [
        pltpu.with_memory_space_constraint(x, pltpu.HBM)
        for x in (clip_lengths, clip_order, features[0], taps_a, taps_b)
    ]
    (tail,) = kernel(
        last_frames,
        [((2, 8, 32, C), BF)],
        [HBM],
        [pltpu.SemaphoreType.DMA((4,))],
    )(stay[2])
    far = shifted(tail, "span", 2)
    packed = ((12 * C, 6 * C), BF)
    wa, wb, own, flags = kernel(
        prepare,
        [packed, packed, ((3, 4, 32, 2 * C), BF), ((4, 8, C), F32)],
        [HBM] * 5,
        [
            pltpu.SMEM((2, 16), jnp.int32),
            pltpu.VMEM((3, 8, 32, C), BF),
            pltpu.VMEM((2, 27, C, C), BF),
            pltpu.SemaphoreType.DMA((9,)),
        ],
    )(*stay)
    near, hidden_near, taps_near = kernel(
        inner_near,
        [((4, 4, 32, 2 * C), BF), ((5, 3, 32, 2 * C), BF), ((3, 4, 16, 3 * C), BF)],
        [VMEM] * 7,
        [pltpu.VMEM((3, 4, 32, C), F32)],
    )(near, own, wa, ba, wb, bb, flags)
    up, far = kernel(
        pack_up, [((9, 3, 32, C), BF), ((2, 4, 32, 2 * C), BF)], [VMEM] * 5
    )(far, near, own, flags, taps_near)
    above = shifted(up, "row", 1)
    (down,) = kernel(pack_down, [((9, 2, 32, C), BF)], [VMEM] * 3)(far, near, own)
    below = shifted(down, "row", -1)
    (hidden_far,) = kernel(inner_far, [((2, 3, 32, 2 * C), BF)], [VMEM] * 5)(far, near, wa, ba, flags)
    (taps_far,) = kernel(
        inner_mixed, [((2, 4, 16, 3 * C), BF)], [VMEM] * 6, [pltpu.VMEM((2, 4, 32, C), F32)]
    )(near, wb, bb, flags, hidden_far, hidden_near)
    sums_hidden = ((7 * 32, 2 * C), F32)
    sums_mixed = ((5 * 32, 2 * C), F32)
    top_hidden, top_mixed, bottom_hidden, bottom_mixed, wlow = kernel(
        early_part, [sums_hidden, sums_mixed] * 2 + [((6 * C, 3 * C), BF)], [VMEM] * 9
    )(far, near, own, wa, wb, wd, hidden_far, hidden_near, taps_far)
    (sums,) = kernel(
        top_part,
        [((128, C), F32)],
        [VMEM] * 15,
        [pltpu.VMEM((7, 2, 32, 2 * C), BF), pltpu.VMEM((5, 3, 32, C), F32)],
    )(far, near, own, above, wa, ba, wb, bb, wd, bd, flags, top_hidden, top_mixed, taps_far, taps_near)
    (out,) = kernel(
        bottom_part,
        [((2, 2, 8, 4 * C), BF)],
        [VMEM] * 13,
        [pltpu.VMEM((7, 32, 2 * C), BF), pltpu.VMEM((5, 2, 32, C), F32)],
    )(far, near, own, below, wa, ba, wb, bb, wlow, flags, bottom_hidden, bottom_mixed, sums)
    return out[None]


def solution(mesh):
    placed = (P("span", None, "row", None, None), P(), P(), P(), P(), P(), P(), P(), P())
    return jax.shard_map(
        per_device,
        mesh=mesh,
        in_specs=placed,
        out_specs=P("span", None, "row", None, None),
        check_vma=False,
    )
```

```python
import jax
import jax.numpy as jnp
from jax import lax
from jax.experimental import pallas as pl
from jax.experimental.pallas import tpu as pltpu
from jax.sharding import PartitionSpec as P

BF = jnp.bfloat16
F32 = jnp.float32
C = 128
VMEM = pl.BlockSpec(memory_space=pltpu.VMEM)
HBM = pl.BlockSpec(memory_space=pltpu.HBM)


def shifted(x, axis, by):
    peers = lax.axis_size(axis)
    pairs = [(i, i + by) for i in range(peers) if 0 <= i + by < peers]
    return lax.ppermute(x, axis, pairs)


def continues(lengths, order, slot):
    begin = jnp.int32(0)
    first = jnp.int32(0)
    for k in range(16):
        first = jnp.where(begin == slot, jnp.int32(1), first)
        begin = begin + lengths[order[k]]
    return 1 - first


def last_frames(features, out, sem):
    copies = [
        pltpu.make_async_copy(features.at[2 + f, pl.ds(4 * part, 4)], out.at[f, pl.ds(4 * part, 4)], sem.at[2 * f + part])
        for f in range(2)
        for part in range(2)
    ]
    for copy in copies:
        copy.start()
    for copy in copies:
        copy.wait()


def prepare(lengths, order, features, a, b, pa, pb, pairs, flags, smem, own, taps, sem):
    copies = [
        pltpu.make_async_copy(lengths, smem.at[0], sem.at[0]),
        pltpu.make_async_copy(order, smem.at[1], sem.at[1]),
        pltpu.make_async_copy(features.at[pl.ds(0, 3)], own, sem.at[2]),
    ]
    for i, src in enumerate((a, b)):
        for t in range(3):
            part = pl.ds(9 * t, 9)
            copies.append(pltpu.make_async_copy(src.at[part], taps.at[i, part], sem.at[3 + 3 * i + t]))
    for copy in copies:
        copy.start()
    for copy in copies[:3]:
        copy.wait()
    slot = lax.axis_index("span")
    block = lax.axis_index("row")
    values = (
        continues(smem.at[0], smem.at[1], slot),
        continues(smem.at[0], smem.at[1], slot - 1),
        (block > 0).astype(jnp.int32),
        (block < lax.axis_size("row") - 1).astype(jnp.int32),
    )
    for i, value in enumerate(values):
        flags[i] = jnp.full((8, C), value.astype(F32), F32)
    for f in range(3):
        for row in range(8):
            pairs[f, row // 2, :, pl.ds(row % 2 * C, C)] = own[f, row]
    for n, dst in enumerate((pa, pb)):
        for t in range(3):
            copies[3 + 3 * n + t].wait()
            for i in range(4):
                for w in range(3):
                    for j in range(2):
                        k = i - j
                        value = taps[n, t * 9 + k * 3 + w] if 0 <= k <= 2 else jnp.zeros((C, C), BF)
                        at = (i // 2 * 3 + t) * 2 + i % 2
                        dst[pl.ds(at * C, C), pl.ds((j * 3 + w) * C, C)] = value


def pack_up(far, near, own, flags, after, up, pairs):
    both = (flags[0, 0:1, :] * flags[1, 0:1, :]).astype(BF)
    for f in range(2):
        for row in range(8):
            value = far[f, row] * both
            pairs[f, row // 2, :, pl.ds(row % 2 * C, C)] = value
            if row >= 5:
                up[f, row - 5] = value
    for f in range(7):
        for row in range(5, 8):
            lanes = pl.ds(row % 2 * C, C)
            up[2 + f, row - 5] = near[f, row // 2, :, lanes] if f < 4 else own[f - 4, row // 2, :, lanes]


def pack_down(far, near, own, down):
    for f in range(9):
        for row in range(2):
            src, at = (far, f) if f < 2 else (near, f - 2) if f < 6 else (own, f - 6)
            down[f, row] = src[at, 0, :, pl.ds(row * C, C)]


def twice(bias):
    return jnp.concatenate([bias[...], bias[...]], axis=1)


def conv(blocks, fetch, weight, sides=(0, 1), lower=False):
    rows = len(blocks) * 32
    lhs = jnp.concatenate(
        [
            jnp.concatenate([fetch(f - 2 + t, q + side) for f, q in blocks], axis=0)
            for side in sides
            for t in range(3)
        ],
        axis=1,
    )
    rhs = weight[pl.ds(sides[0] * 6 * C, len(sides) * 6 * C), pl.ds(3 * C if lower else 0, 3 * C if lower else 6 * C)]
    y = jnp.dot(lhs, rhs, preferred_element_type=F32).reshape(len(blocks), 32, -1)
    col = lax.broadcasted_iota(jnp.int32, (1, 32, C), 1)
    out = []
    for at in range(0, y.shape[2], 3 * C):
        left = jnp.where(col == 0, 0.0, pltpu.roll(y[:, :, at : at + C], 1, 1))
        right = jnp.where(col == 31, 0.0, pltpu.roll(y[:, :, at + 2 * C : at + 3 * C], 31, 1))
        out.append(y[:, :, at + C : at + 2 * C] + left + right)
    return (out[0] if lower else jnp.concatenate(out, axis=2)).reshape(rows, -1)


def hidden_blocks(blocks, sums, bias, flags, put):
    lower = sums.shape[1] == C
    v = sums + (bias[...] if lower else twice(bias))
    v = v / (1.0 + jnp.exp(-v))
    keep, top, bottom = (flags[i, 0:1, :] for i in (0, 2, 3))
    one = jnp.ones_like(top)
    for i, (f, q) in enumerate(blocks):
        value = v[i * 32 : i * 32 + 32]
        if q == 0:
            value = value * top
        elif q == 1:
            value = value * jnp.concatenate([top, one], axis=1)
        elif q == 5:
            value = value * jnp.concatenate([one, bottom], axis=1)
        if f < 0:
            value = value * (keep if lower else jnp.concatenate([keep, keep], axis=1))
        put(f, q, value.astype(BF))


def mixed_blocks(blocks, sums, residual, bias, flags, put):
    lower = sums.shape[1] == C
    v = sums + (bias[...] if lower else twice(bias))
    keep, top = flags[0, 0:1, :], flags[2, 0:1, :]
    for i, (f, p) in enumerate(blocks):
        x = residual(f, p + 1).astype(F32)
        value = (x[:, C:] if lower else x) + v[i * 32 : i * 32 + 32]
        value = value.astype(BF).astype(F32)
        if f < 0:
            value = value * (keep if lower else jnp.concatenate([keep, keep], axis=1))
        if p == 0:
            put(f, 0, value * top)
        else:
            put(f, 2 * p - 1, value[:, :C])
            put(f, 2 * p, value[:, C:])


def column_taps(row):
    m = [row[pl.ds(k, 8, stride=4), :] for k in range(4)]
    first = lax.broadcasted_iota(jnp.int32, (8, C), 0) == 0
    before = jnp.where(first, 0.0, pltpu.roll(m[3], 1, 0))
    columns = ((before, m[1]), (m[0], m[2]), (m[1], m[3]))
    return jnp.concatenate([jnp.concatenate(pair, axis=0).astype(BF) for pair in columns], axis=1)


def own_feature(far, near, own):
    def feature(f, g):
        src, at = (far, f + 6) if f < -4 else (near, f + 4) if f < 0 else (own, f)
        return src[at, g - 2]

    return feature


def inner_near(arrived, own, wa, ba, wb, bb, flags, near, hidden, taps, m):
    keep = flags[0, 0:1, :].astype(BF)
    for f in range(4):
        for row in range(8):
            near[f, row // 2, :, pl.ds(row % 2 * C, C)] = arrived[f, row] * keep
    feature = own_feature(None, near, own)

    def put_hidden(f, q, value):
        hidden[f + 2, q - 2] = value

    def put_mixed(f, r, value):
        m[f, r - 3] = value

    for frames in ((-2, -1), (0, 1, 2)):
        blocks = [(f, q) for f in frames for q in (2, 3, 4)]
        hidden_blocks(blocks, conv(blocks, feature, wa), ba, flags, put_hidden)
    blocks = [(f, p) for f in range(3) for p in (2, 3)]
    sums = conv(blocks, lambda f, q: hidden[f + 2, q - 2], wb)
    mixed_blocks(blocks, sums, feature, bb, flags, put_mixed)
    for f in range(3):
        for r in range(4):
            taps[f, r] = column_taps(m.at[f, r])


def inner_far(far, near, wa, ba, flags, hidden):
    def put_hidden(f, q, value):
        hidden[f + 4, q - 2] = value

    blocks = [(f, q) for f in (-4, -3) for q in (2, 3, 4)]
    hidden_blocks(blocks, conv(blocks, own_feature(far, near, None), wa), ba, flags, put_hidden)


def inner_mixed(near, wb, bb, flags, hidden_far, hidden_near, taps, m):
    def hidden(f, q):
        return hidden_far[f + 4, q - 2] if f < -2 else hidden_near[f + 2, q - 2]

    def put_mixed(f, r, value):
        m[f + 2, r - 3] = value

    blocks = [(f, p) for f in (-2, -1) for p in (2, 3)]
    mixed_blocks(blocks, conv(blocks, hidden, wb), own_feature(None, near, None), bb, flags, put_mixed)
    for f in range(2):
        for r in range(4):
            taps[f, r] = column_taps(m.at[f, r])


HIDDEN = range(-4, 3)
MIXED = range(-2, 3)


def inner_hidden(hidden_far, hidden_near):
    def hidden(f, q):
        return hidden_far[f + 4, q - 2] if f < -2 else hidden_near[f + 2, q - 2]

    return hidden


def early_part(
    far, near, own, wa, wb, wd, hidden_far, hidden_near, after, top_hidden, top_mixed, bottom_hidden, bottom_mixed, low
):
    feature = own_feature(far, near, own)
    hidden = inner_hidden(hidden_far, hidden_near)
    top_hidden[...] = conv([(f, 1) for f in HIDDEN], feature, wa, (1,))
    top_mixed[...] = conv([(f, 1) for f in MIXED], hidden, wb, (1,))
    bottom_hidden[...] = conv([(f, 5) for f in HIDDEN], feature, wa, (0,))
    bottom_mixed[...] = conv([(f, 4) for f in MIXED], hidden, wb, (0,))
    for t in range(3):
        low[:, pl.ds(t * C, C)] = wd[pl.ds((9 * t + 3) * C, 6 * C), :]


def top_part(
    far, near, own, above, wa, ba, wb, bb, wd, bd, flags, part_hidden, part_mixed, taps_far, taps_near, sums, h, m
):
    inside = own_feature(far, near, own)

    def feature(f, g):
        if g >= 2:
            return inside(f, g)
        upper = jnp.zeros((32, C), BF) if g == 0 else above[f + 6, 1]
        return jnp.concatenate([upper, above[f + 6, 2 * g]], axis=1)

    def put_hidden(f, q, value):
        if q == 0:
            h[f + 4, 0, :, pl.ds(0, C)] = jnp.zeros((32, C), BF)
            h[f + 4, 0, :, pl.ds(C, C)] = value
        else:
            h[f + 4, 1] = value

    def put_mixed(f, r, value):
        m[f + 2, r] = value

    def hidden(f, q):
        return h[f + 4, q]

    blocks = [(f, 1) for f in HIDDEN]
    hidden_blocks(blocks, conv(blocks, feature, wa, (0,)) + part_hidden[...], ba, flags, put_hidden)
    blocks = [(f, 0) for f in HIDDEN]
    hidden_blocks(blocks, conv(blocks, feature, wa, lower=True), ba, flags, put_hidden)
    blocks = [(f, 1) for f in MIXED]
    mixed_blocks(blocks, conv(blocks, hidden, wb, (0,)) + part_mixed[...], feature, bb, flags, put_mixed)
    ready = [[column_taps(m.at[f, r]) for r in (1, 2)] for f in range(5)]
    blocks = [(f, 0) for f in MIXED]
    mixed_blocks(blocks, conv(blocks, hidden, wb, lower=True), feature, bb, flags, put_mixed)
    none = jnp.zeros((16, 3 * C), BF)
    frames = []
    for f in range(5):
        rows = [column_taps(m.at[f, 0])] + ready[f]
        rows += [taps_far[f, r] if f < 2 else taps_near[f - 2, r] for r in range(4)] + [none, none]
        frames.append(
            jnp.concatenate(
                [jnp.concatenate([rows[2 * j + k] for k in range(3)], axis=1) for j in range(4)], axis=0
            )
        )
    lhs = jnp.concatenate([jnp.concatenate(frames[t : t + 3], axis=1) for t in (0, 2)], axis=0)
    sums[...] = jnp.dot(lhs, wd[...], preferred_element_type=F32) + bd[...]


def bottom_part(
    far, near, own, below, wa, ba, wb, bb, wlow, flags, part_hidden, part_mixed, sums, out, h, m
):
    def feature(f, g):
        return jnp.concatenate([below[f + 6, 0], below[f + 6, 1]], axis=1)

    def put_hidden(f, q, value):
        h[f + 4] = value

    def put_mixed(f, r, value):
        m[f + 2, r - 7] = value

    blocks = [(f, 5) for f in HIDDEN]
    hidden_blocks(blocks, conv(blocks, feature, wa, (1,)) + part_hidden[...], ba, flags, put_hidden)
    blocks = [(f, 4) for f in MIXED]
    total = conv(blocks, lambda f, q: h[f + 4], wb, (1,)) + part_mixed[...]
    mixed_blocks(blocks, total, own_feature(far, near, own), bb, flags, put_mixed)
    rows = [jnp.concatenate([column_taps(m.at[f, r]) for r in range(2)], axis=1) for f in range(5)]
    y = jnp.dot(jnp.concatenate(rows, axis=0), wlow[...], preferred_element_type=F32)
    low = [sum(y[(2 * t + k) * 16 : (2 * t + k) * 16 + 16, k * C : k * C + C] for k in range(3)) for t in range(2)]
    for t in range(2):
        for i in range(2):
            at = t * 64 + i * 32
            v = sums[at : at + 32]
            if i == 1:
                v = jnp.concatenate([v[:16], v[16:] + low[t]], axis=0)
            out[t, i] = jnp.concatenate([v[k * 8 : k * 8 + 8] for k in range(4)], axis=1).astype(BF)


def kernel(body, outs, ins, scratch=(), flops=0):
    return pl.pallas_call(
        body,
        name=body.__name__,
        out_shape=[jax.ShapeDtypeStruct(*o) for o in outs],
        in_specs=ins,
        out_specs=[VMEM] * len(outs),
        scratch_shapes=list(scratch),
        compiler_params=pltpu.CompilerParams(vmem_limit_bytes=24 << 20),
        cost_estimate=pl.CostEstimate(flops=flops, bytes_accessed=1 << 10, transcendentals=0),
    )


def per_device(
    features, clip_lengths, clip_order, weight_a, bias_a, weight_b, bias_b, weight_down, bias_down
):
    wd = weight_down.reshape(27 * C, C)
    ba, bb, bd = (b.reshape(1, C) for b in (bias_a, bias_b, bias_down))
    near = shifted(features[0], "span", 1)
    taps_a, taps_b = (w.reshape(27, C, C) for w in (weight_a, weight_b))
    stay = [
        pltpu.with_memory_space_constraint(x, pltpu.HBM)
        for x in (clip_lengths, clip_order, features[0], taps_a, taps_b)
    ]
    (tail,) = kernel(
        last_frames,
        [((2, 8, 32, C), BF)],
        [HBM],
        [pltpu.SemaphoreType.DMA((4,))],
    )(stay[2])
    far = shifted(tail, "span", 2)
    packed = ((12 * C, 6 * C), BF)
    wa, wb, own, flags = kernel(
        prepare,
        [packed, packed, ((3, 4, 32, 2 * C), BF), ((4, 8, C), F32)],
        [HBM] * 5,
        [
            pltpu.SMEM((2, 16), jnp.int32),
            pltpu.VMEM((3, 8, 32, C), BF),
            pltpu.VMEM((2, 27, C, C), BF),
            pltpu.SemaphoreType.DMA((9,)),
        ],
    )(*stay)
    near, hidden_near, taps_near = kernel(
        inner_near,
        [((4, 4, 32, 2 * C), BF), ((5, 3, 32, 2 * C), BF), ((3, 4, 16, 3 * C), BF)],
        [VMEM] * 7,
        [pltpu.VMEM((3, 4, 32, C), F32)],
    )(near, own, wa, ba, wb, bb, flags)
    up, far = kernel(
        pack_up, [((9, 3, 32, C), BF), ((2, 4, 32, 2 * C), BF)], [VMEM] * 5
    )(far, near, own, flags, taps_near)
    above = shifted(up, "row", 1)
    (down,) = kernel(pack_down, [((9, 2, 32, C), BF)], [VMEM] * 3)(far, near, own)
    below = shifted(down, "row", -1)
    (hidden_far,) = kernel(inner_far, [((2, 3, 32, 2 * C), BF)], [VMEM] * 5)(far, near, wa, ba, flags)
    (taps_far,) = kernel(
        inner_mixed, [((2, 4, 16, 3 * C), BF)], [VMEM] * 6, [pltpu.VMEM((2, 4, 32, C), F32)]
    )(near, wb, bb, flags, hidden_far, hidden_near)
    sums_hidden = ((7 * 32, 2 * C), F32)
    sums_mixed = ((5 * 32, 2 * C), F32)
    top_hidden, top_mixed, bottom_hidden, bottom_mixed, wlow = kernel(
        early_part, [sums_hidden, sums_mixed] * 2 + [((6 * C, 3 * C), BF)], [VMEM] * 9
    )(far, near, own, wa, wb, wd, hidden_far, hidden_near, taps_far)
    (sums,) = kernel(
        top_part,
        [((128, C), F32)],
        [VMEM] * 15,
        [pltpu.VMEM((7, 2, 32, 2 * C), BF), pltpu.VMEM((5, 3, 32, C), F32)],
    )(far, near, own, above, wa, ba, wb, bb, wd, bd, flags, top_hidden, top_mixed, taps_far, taps_near)
    (out,) = kernel(
        bottom_part,
        [((2, 2, 8, 4 * C), BF)],
        [VMEM] * 13,
        [pltpu.VMEM((7, 32, 2 * C), BF), pltpu.VMEM((5, 2, 32, C), F32)],
    )(far, near, own, below, wa, ba, wb, bb, wlow, flags, bottom_hidden, bottom_mixed, sums)
    return out[None]


def solution(mesh):
    placed = (P("span", None, "row", None, None), P(), P(), P(), P(), P(), P(), P(), P())
    return jax.shard_map(
        per_device,
        mesh=mesh,
        in_specs=placed,
        out_specs=P("span", None, "row", None, None),
        check_vma=False,
    )
```
